32 devices in a mesh: frames: 2 (over y), az: 4 (over z), rg: 2 (over x), cplx: 2 (over core).
Axes of the slice: x: 2, y: 2, z: 4, core: 2. Of those that a mesh axis runs over, the one named last changes fastest.
Arguments:
- image: bfloat16 [2048, 2, 1024], P(('frames', 'cplx'), None, ('az', 'rg')), parts along dimension 0, may hold values from -6 to 6
- echoes: bfloat16 [2048, 2, 1024], P(('frames', 'cplx'), None, ('az', 'rg')), parts along dimension 0, may hold values from -6 to 6
- slot_time: int32 [2048], P(('frames', 'az', 'rg')), parts along dimension 0, may hold values from -1 to 1023, as said below
- range_matrix: bfloat16 [2, 1024, 1024], P(None, 'cplx'), may hold values from -0.125 to 0.125
- filter_bank: bfloat16 [16, 2, 512], replicated, may hold values from -0.1875 to 0.1875
- filter_index: int32 [1024], replicated, may hold values from 0 to 15
Outputs:
- gradient: float32 [2048, 2, 1024], P(('frames', 'cplx'), None, ('az', 'rg')), parts along dimension 0
The draws below stay inside these ranges and needn't reach their ends.
There are 2 independent parts, one for each index of `frames`. The reference program is written for one: setup_inputs(seed, part) draws one part's arguments, and reference() takes and returns one part's arrays. A program takes and returns all parts, laid end to end along the dimension named above; an argument that names none is the same for every part. Nothing has to cross between parts.
Inputs may be any that keep to these rules, and one draw needn't show every extreme that they name: `slot_time`: owner o holds slots o * 128 to o * 128 + 127: first the azimuth cells of its echo lines, distinct, increasing and within o * 128 to o * 128 + 127, then -1 in every unused slot. Each owner has at least 64 lines, some owner uses all 128 slots, and the last cell 1024 - 1 always has an echo line.
All inputs are finite; a program needn't handle non-finite values.
Results may differ from the reference program's by a relative error of at most 0.0043.
Values may be sent and summed in bfloat16 or wider, within the bound.
No kernel may reach another device: no remote copies, remote signals or barrier semaphores. Data moves between devices by JAX's collectives and lax.ppermute only.
A program may use at most 192 MiB of HBM per device.

```python
import jax
import jax.numpy as jnp
from jax import lax

NR = 1024
L = 512
NB = 16
A_LOC = 128
OWNERS = 8
NA = 1024
CAP = 128
SLOTS = 1024


def draw_slot_time(key, part):
    count_key = jax.random.fold_in(key, 11)
    fullest_key = jax.random.fold_in(key, 12)
    order_key = jax.random.fold_in(key, 13)
    line_counts = jax.random.randint(count_key, (OWNERS,), CAP // 2, CAP)
    fullest = jax.random.randint(fullest_key, (), 0, OWNERS)
    line_counts = jnp.where(jnp.arange(OWNERS) == fullest, CAP, line_counts)
    owner_keys = jax.random.split(order_key, OWNERS)

    def one_owner(owner_key, owner_index, line_count):
        full_order = jax.random.permutation(owner_key, A_LOC)
        first_value = full_order[0]
        swapped = jnp.where(full_order == A_LOC - 1, first_value, full_order)
        swapped = jnp.where(jnp.arange(A_LOC) == 0, A_LOC - 1, swapped)
        pick_order = jnp.where(owner_index == OWNERS - 1, swapped, full_order)[:CAP]
        slot_index = jnp.arange(CAP)
        chosen = jnp.sort(jnp.where(slot_index < line_count, pick_order, A_LOC))
        return jnp.where(slot_index < line_count, chosen + owner_index * A_LOC, -1)
    drawn = jax.vmap(one_owner)(owner_keys, jnp.arange(OWNERS), line_counts)
    return drawn.reshape(OWNERS * CAP).astype(jnp.int32)


def set_ends(array, own_key, low, largest):
    longest = array.shape.index(max(array.shape))
    spots = []
    for shift in (0, 1):
        where = [jax.random.randint(jax.random.fold_in(own_key, axis), (), 0, length) for axis, length in enumerate(array.shape)]
        where[longest] = (where[longest] + shift) % array.shape[longest]
        spots.append(tuple(where))
    return array.at[spots[0]].set(low).at[spots[1]].set(largest)


def levels(own_key, dims, shards, least, top_value):
    factor_of, own = 1.0, jax.random.fold_in(own_key, 6)
    for dim, shards_of in shards:
        steps = jnp.exp(jax.random.uniform(jax.random.fold_in(own, dim), (shards_of,), jnp.float32, least / len(shards), top_value / len(shards)))
        factor_of = factor_of * jnp.repeat(steps, dims[dim] // shards_of).reshape([-1 if axis == dim else 1 for axis in range(len(dims))])
    return factor_of


def scatter_about(stream_key, shape, scale, most, pieces=(), kind=jnp.bfloat16):
    factor_of = levels(stream_key, shape, pieces, -0.22, 0.18) if pieces else 1.0
    array = jax.random.normal(stream_key, shape, jnp.float32) * scale * factor_of
    return jnp.minimum(jnp.maximum(array, -most), most).astype(kind)


def setup_inputs(seed: int = 0, part: int = 0) -> dict:
    splits = jax.random.split(jax.random.key(seed), 7)
    part_splits = jax.random.split(jax.random.fold_in(splits[6], part), 7)
    return {
        "image": scatter_about(part_splits[0], (NR, 2, NA), 1.0, 6.0, ((0, 2), (2, 8))),
        "echoes": scatter_about(part_splits[1], (NR, 2, SLOTS), 1.0, 6.0, ((0, 2), (2, 8))),
        "slot_time": draw_slot_time(jax.random.fold_in(jax.random.fold_in(splits[6], part), 71), part),
        "range_matrix": scatter_about(splits[3], (2, NR, NR), (2 * NR) ** -0.5, 0.125, ((1, 2),)),
        "filter_bank": scatter_about(splits[4], (NB, 2, L), (2 * L) ** -0.5, 0.1875),
        "filter_index": set_ends(jax.random.randint(splits[5], (NR,), 0, NB), jax.random.fold_in(splits[5], 1), 0, NB - 1).astype(jnp.int32),
    }


def band_matrix(filter_taps):
    tap_count = filter_taps.shape[-1]
    lead_shape = filter_taps.shape[:-1]
    padded = jnp.concatenate([filter_taps, jnp.zeros(lead_shape + (tap_count + 1,), filter_taps.dtype)], axis=-1)
    tiled_taps = jnp.tile(padded, (1,) * len(lead_shape) + (tap_count,))
    return tiled_taps[..., : 2 * tap_count * tap_count].reshape(lead_shape + (tap_count, 2 * tap_count))


def forward_line(signal, toeplitz):
    tap_count = toeplitz.shape[1]
    cell_count = signal.shape[1]
    block_count = cell_count // tap_count
    half_taps = tap_count // 2
    padded = jnp.pad(signal, ((0, 0), (half_taps, tap_count - half_taps)))
    windows = jnp.concatenate([padded[:, :cell_count].reshape(2, block_count, tap_count), padded[:, tap_count:].reshape(2, block_count, tap_count)], axis=2).reshape(2 * block_count, 2 * tap_count)
    contract_dims = (((1,), (1,)), ((), ()))
    real_part = lax.dot_general(windows, toeplitz[0], contract_dims, preferred_element_type=jnp.float32)
    imag_part = lax.dot_general(windows, toeplitz[1], contract_dims, preferred_element_type=jnp.float32)
    out_real = real_part[:block_count] - imag_part[block_count:]
    out_imag = real_part[block_count:] + imag_part[:block_count]
    return jnp.stack([out_real.reshape(cell_count), out_imag.reshape(cell_count)]).astype(jnp.bfloat16)


def adjoint_line(signal, toeplitz):
    tap_count = toeplitz.shape[1]
    cell_count = signal.shape[1]
    block_count = cell_count // tap_count
    half_taps = tap_count // 2
    blocked = signal.reshape(2 * block_count, tap_count)
    real_part = jnp.dot(blocked, toeplitz[0], preferred_element_type=jnp.float32)
    imag_part = jnp.dot(blocked, toeplitz[1], preferred_element_type=jnp.float32)
    out_real = real_part[:block_count] + imag_part[block_count:]
    out_imag = real_part[block_count:] - imag_part[:block_count]
    stacked = jnp.stack([out_real, out_imag])
    head_part = stacked[:, :, :tap_count].reshape(2, cell_count)
    tail_part = stacked[:, :, tap_count:].reshape(2, cell_count)
    summed = jnp.pad(head_part, ((0, 0), (0, tap_count))) + jnp.pad(tail_part, ((0, 0), (tap_count, 0)))
    return summed[:, half_taps: half_taps + cell_count].astype(jnp.bfloat16)


def reference(image, echoes, slot_time, range_matrix, filter_bank, filter_index):
    bin_count = image.shape[0]
    cell_count = image.shape[2]
    flat_image = image.reshape(bin_count, 2 * cell_count)
    from_real = jnp.dot(range_matrix[0], flat_image, preferred_element_type=jnp.float32)
    from_imag = jnp.dot(range_matrix[1], flat_image, preferred_element_type=jnp.float32)
    compressed = jnp.stack([from_real[:, :cell_count] - from_imag[:, cell_count:], from_real[:, cell_count:] + from_imag[:, :cell_count]], axis=1).astype(jnp.bfloat16)
    filter_taps = filter_bank[filter_index]
    model = lax.map(lambda member: forward_line(member[0], band_matrix(member[1])), (compressed, filter_taps))
    target_cell = jnp.where(slot_time < 0, cell_count, slot_time)
    occupied = jnp.zeros((cell_count,), jnp.float32).at[target_cell].set(1.0, mode="drop")
    echo_grid = jnp.zeros((bin_count, 2, cell_count), jnp.bfloat16).at[:, :, target_cell].set(echoes, mode="drop")
    residual = (occupied * model.astype(jnp.float32) - echo_grid.astype(jnp.float32)).astype(jnp.bfloat16)
    back = lax.map(lambda member: adjoint_line(member[0], band_matrix(member[1])), (residual, filter_taps))
    flat_back = back.reshape(bin_count, 2 * cell_count)
    back_real = jnp.dot(range_matrix[0].T, flat_back, preferred_element_type=jnp.float32)
    back_imag = jnp.dot(range_matrix[1].T, flat_back, preferred_element_type=jnp.float32)
    gradient = jnp.stack([back_real[:, :cell_count] + back_imag[:, cell_count:], back_real[:, cell_count:] - back_imag[:, :cell_count]], axis=1)
    return gradient
```

```python
import functools

import jax
import jax.numpy as jnp
from jax import lax
from jax.experimental import pallas as pl
from jax.experimental.pallas import tpu as pltpu
from jax.sharding import PartitionSpec as P

GROUP = 32
F32 = jnp.float32
BF16 = jnp.bfloat16
VMEM = pl.BlockSpec(memory_space=pltpu.VMEM)
SMEM = pl.BlockSpec(memory_space=pltpu.SMEM)


def mm(a, b):
    return jnp.dot(a, b, preferred_element_type=F32)


def mm_nt(a, b):
    return lax.dot_general(a, b, (((1,), (1,)), ((), ())), preferred_element_type=F32)


def mm_tn(a, b):
    return lax.dot_general(a, b, (((0,), (0,)), ((), ())), preferred_element_type=F32)


def iota(shape, axis):
    return lax.broadcasted_iota(jnp.int32, shape, axis)


def column_of(row):
    size = row.shape[1]
    eye = iota((size, size), 0) == iota((size, size), 1)
    return jnp.sum(jnp.where(eye, jnp.broadcast_to(row, (size, size)), 0.0), axis=1, keepdims=True)


def part_of(count, step):
    return lax.axis_index("rg") ^ step if count == 2 else step


def call(body, out_shape, in_specs, scratch=(), flops=0, out_specs=None, limit=None):
    count = sum(x.size * x.dtype.itemsize for x in jax.tree.leaves(out_shape))
    return pl.pallas_call(
        body,
        out_shape=out_shape,
        in_specs=in_specs,
        out_specs=jax.tree.map(lambda _: VMEM, out_shape) if out_specs is None else out_specs,
        scratch_shapes=list(scratch),
        cost_estimate=pl.CostEstimate(flops=flops, bytes_accessed=count, transcendentals=0),
        compiler_params=pltpu.CompilerParams(vmem_limit_bytes=limit or 50 * 2**20),
    )


def prep_body(parts, bank, cell_count, index_ref, echo_ref, time_ref, starts_ref, perm_ref, back_ref, *rest):
    echo_out, tmp_ref = rest[:parts], rest[parts]
    bins = index_ref.shape[1]
    owner = lax.axis_index("az") * parts + lax.axis_index("rg")
    half = lax.axis_index("cplx")
    local = (time_ref[...] - owner * cell_count).astype(F32)
    slots = local.shape[1]
    hits = column_of(local) == iota((slots, cell_count), 1).astype(F32)
    place = hits.astype(BF16)
    occupied = jnp.sum(hits.astype(F32), axis=0, keepdims=True)
    for step in range(parts):
        part = part_of(parts, step)
        ids = index_ref[pl.ds(half * parts + part, 1), :]
        key = (ids * bins + iota((1, bins), 1)).astype(F32)
        rank = jnp.sum((column_of(key) < key).astype(F32), axis=0, keepdims=True)
        perm = (iota((bins, bins), 0).astype(F32) == rank).astype(BF16)
        perm_ref[step] = perm
        rows = echo_ref[pl.ds(pl.multiple_of(part * 2 * bins, 2 * bins), 2 * bins), :]
        tmp_ref[...] = mm(rows, place)
        split = jnp.concatenate(
            [tmp_ref[pl.ds(0, bins, stride=2), :], tmp_ref[pl.ds(1, bins, stride=2), :]], axis=1
        ).astype(BF16)
        moved = mm(perm, split).astype(BF16)
        echo_out[step][0:bins, :] = moved[:, :cell_count]
        echo_out[step][bins : 2 * bins, :] = moved[:, cell_count:]
        echo_out[step][2 * bins :, :] = jnp.broadcast_to(occupied, (16, cell_count)).astype(BF16)
    own = lax.axis_index("rg")
    ids = index_ref[pl.ds(half * parts + own, 1), :]
    key = (ids * bins + iota((1, bins), 1)).astype(F32)
    rank = jnp.sum((column_of(key) < key).astype(F32), axis=0, keepdims=True)
    back_ref[...] = (column_of(rank) == iota((bins, bins), 1).astype(F32)).astype(BF16)
    for number in range(bank + 1):
        starts_ref[number] = jnp.sum((ids < number).astype(F32)).astype(jnp.int32)


def bands_body(seg, bank_ref, fwd_ref, adj_ref):
    taps = bank_ref.shape[2]
    width = taps + seg
    pad = jnp.zeros((1, seg), F32)
    for part in range(2):
        row = jnp.concatenate([bank_ref[0, part : part + 1, :].astype(F32), pad], axis=1)
        rolled = pltpu.roll(jnp.broadcast_to(row, (seg, width)), 0, 1, stride=1, stride_axis=0)
        rolled = rolled.astype(BF16)
        fwd_ref[0, part * seg : (part + 1) * seg, :] = rolled
        count = width // seg
        for block in range(count):
            adj_ref[0, block * seg : (block + 1) * seg, part * seg : (part + 1) * seg] = rolled[
                :, (count - 1 - block) * seg : (count - block) * seg
            ]


def compress_body(parts, own_ref, other_ref, matrix_ref, perm_ref, *rest):
    outs, tmp_ref, image_ref = rest[:parts], rest[parts], rest[parts + 1]
    half = lax.axis_index("cplx")
    rows_own, cells = own_ref.shape[0] // 2, own_ref.shape[1]
    bins = perm_ref.shape[1]
    for ref, at in ((own_ref, half), (other_ref, 1 - half)):
        tmp_ref[...] = ref[...].astype(F32)
        rows = pl.ds(pl.multiple_of(at * rows_own, rows_own), rows_own)
        image_ref[rows, :cells] = tmp_ref[pl.ds(0, rows_own, stride=2), :].astype(BF16)
        image_ref[rows, cells:] = tmp_ref[pl.ds(1, rows_own, stride=2), :].astype(BF16)
    for step in range(parts):
        rows = pl.ds(pl.multiple_of(part_of(parts, step) * bins, bins), bins)
        from_real = mm(matrix_ref[0, rows, :], image_ref[...])
        from_imag = mm(matrix_ref[1, rows, :], image_ref[...])
        real = from_real[:, :cells] - from_imag[:, cells:]
        imag = from_real[:, cells:] + from_imag[:, :cells]
        sent = mm(perm_ref[step], jnp.concatenate([real, imag], axis=1).astype(BF16)).astype(BF16)
        outs[step][:bins, :] = sent[:, :cells]
        outs[step][bins:, :] = sent[:, cells:]


def fill_blocks(blocks_ref, pieces):
    for ref, at in pieces:
        if len(ref.shape) == 2:
            blocks_ref[at] = ref[...]
        else:
            for number in range(ref.shape[0]):
                blocks_ref[at + number] = ref[number]


def side_bases(parts, halo):
    even = lax.rem(lax.axis_index("az"), 2) == 0
    right = halo + parts
    return jnp.where(even, right, 0), jnp.where(even, 0, right)


def filter_groups(starts_ref, bank, bins, group, work):
    def per_filter(number, carry):
        low, high = starts_ref[number], starts_ref[number + 1]

        def per_group(at, carry):
            first = pl.multiple_of(at * group, group)
            slot = iota((group, 1), 0) + first
            work(number, first, (slot >= low) & (slot < high))
            return carry

        stop = jnp.where(high > low, lax.div(high + (group - 1), group), lax.div(low, group))
        return lax.fori_loop(lax.div(low, group), stop, per_group, carry)

    lax.fori_loop(0, bank, per_filter, 0)


def windows(blocks_ref, parts, first, group, bins, span):
    cells = blocks_ref.shape[2]
    loaded = [
        [blocks_ref[block, pl.ds(side * bins + first, group), :] for block in range(blocks_ref.shape[0])]
        for side in range(2)
    ]
    return jnp.concatenate(
        [
            jnp.concatenate(loaded[side][block : block + span], axis=1)
            for block in range(parts)
            for side in range(2)
        ],
        axis=0,
    )


def forward_body(parts, halo, names, starts_ref, *rest):
    count = len(names)
    pieces, bands_ref = rest[:count], rest[count]
    echoes = rest[count + 1 : -3]
    out_ref, blocks_ref, sum_ref = rest[-3:]
    bank, cells = bands_ref.shape[0], blocks_ref.shape[2]
    bins = blocks_ref.shape[1] // 2
    span = bands_ref.shape[2] // cells
    group = min(GROUP, bins)
    even_base, odd_base = side_bases(parts, halo)
    base = {"even": even_base, "odd": odd_base, "own": halo}
    fill_blocks(blocks_ref, [(ref, base[side] + (part_of(parts, step) if parts == 2 else step)) for ref, (side, step) in zip(pieces, names)])

    def work(number, first, mask):
        made = mm_nt(windows(blocks_ref, parts, first, group, bins, span), bands_ref[number])
        for block in range(parts):
            top = made[2 * block * group : (2 * block + 1) * group]
            low = made[(2 * block + 1) * group : (2 * block + 2) * group]
            for side, value in enumerate((top[:, :cells] - low[:, cells:], top[:, cells:] + low[:, :cells])):
                rows = pl.ds(side * bins + first, group)
                sum_ref[block, rows, :] = jnp.where(mask, value, sum_ref[block, rows, :])

    filter_groups(starts_ref, bank, bins, group, work)
    for step in range(parts):
        part = part_of(parts, step)
        echo = echoes[step][...] if len(echoes) > 1 else echoes[0][step]
        occupied = echo[2 * bins : 2 * bins + 1].astype(F32)
        model = sum_ref[part].astype(BF16).astype(F32)
        out_ref[part] = (occupied * model - echo[: 2 * bins].astype(F32)).astype(BF16)


def adjoint_body(parts, halo, starts_ref, even_ref, own_ref, odd_ref, bands_ref, perm_ref, *rest):
    outs, (blocks_ref, sum_ref) = rest[:parts], rest[parts:]
    bank, cells = bands_ref.shape[0], blocks_ref.shape[2]
    bins = blocks_ref.shape[1] // 2
    span = bands_ref.shape[1] // cells
    group = min(GROUP, bins)
    even_base, odd_base = side_bases(parts, halo)
    fill_blocks(blocks_ref, [(even_ref, even_base), (own_ref, halo), (odd_ref, odd_base)])

    def work(number, first, mask):
        made = mm(windows(blocks_ref, parts, first, group, bins, span), bands_ref[number])
        for block in range(parts):
            top = made[2 * block * group : (2 * block + 1) * group]
            low = made[(2 * block + 1) * group : (2 * block + 2) * group]
            for side, value in enumerate((top[:, :cells] + low[:, cells:], low[:, :cells] - top[:, cells:])):
                rows = pl.ds(side * bins + first, group)
                sum_ref[block, rows, :] = jnp.where(mask, value, sum_ref[block, rows, :])

    filter_groups(starts_ref, bank, bins, group, work)
    for step in range(parts):
        part = part_of(parts, step)
        both = jnp.concatenate([sum_ref[part, :bins, :], sum_ref[part, bins:, :]], axis=1).astype(BF16)
        both = mm(perm_ref[...], both).astype(BF16)
        outs[step][:bins, :] = both[:, :cells]
        outs[step][bins:, :] = both[:, cells:]


def gradient_body(parts, *refs):
    count = (len(refs) - 5) // 2
    own, other = refs[:count], refs[count : 2 * count]
    matrix_ref, moved_ref, out_ref, real_ref, imag_ref = refs[2 * count :]
    rows_own = matrix_ref.shape[1]
    cells = own[0].shape[-1]
    bins = rows_own // parts
    half = lax.axis_index("cplx")
    columns = pl.ds(pl.multiple_of(half * rows_own, rows_own), rows_own)
    first = True
    for pieces, mine in ((own, True), (other, False)):
        for step in range(parts):
            piece = pieces[step][...] if count > 1 else pieces[0][step]
            both = jnp.concatenate([piece[:bins], piece[bins:]], axis=1)
            rows = pl.ds(pl.multiple_of(part_of(parts, step) * bins, bins), bins)
            if mine:
                real, imag = matrix_ref[0, rows, columns], matrix_ref[1, rows, columns]
            else:
                real, imag = moved_ref[0, rows, :], moved_ref[1, rows, :]
            from_real, from_imag = mm_tn(both, real), mm_tn(both, imag)
            if first:
                real_ref[...], imag_ref[...] = from_real, from_imag
            else:
                real_ref[...] += from_real
                imag_ref[...] += from_imag
            first = False
    grad_real = real_ref[:cells, :] + imag_ref[cells:, :]
    grad_imag = real_ref[cells:, :] - imag_ref[:cells, :]
    out_ref[pl.ds(0, rows_own, stride=2), :] = grad_real.T
    out_ref[pl.ds(1, rows_own, stride=2), :] = grad_imag.T


def swap_pairs(count, first):
    pairs = []
    for low in range(first, count - 1, 2):
        pairs += [(low, low + 1), (low + 1, low)]
    return pairs


def on_device(image, echoes, slot_time, range_matrix, filter_bank, filter_index):
    rows_own, _, cells = image.shape
    parts, rows_az = lax.axis_size("rg"), lax.axis_size("az")
    bins = rows_own // parts
    bank, _, taps = filter_bank.shape
    halo = taps // 2 // cells
    span = taps // cells + 1
    half = lax.axis_index("cplx")
    flip = [(0, 1), (1, 0)]
    struct = jax.ShapeDtypeStruct
    even_pairs, odd_pairs = swap_pairs(rows_az, 0), swap_pairs(rows_az, 1)

    def halves(x):
        return lax.ppermute(x, "cplx", flip)

    def share(pieces):
        if parts == 2:
            return [pieces[0], lax.ppermute(pieces[1], "rg", flip)]
        return [lax.all_to_all(jnp.stack(pieces), "rg", split_axis=0, concat_axis=0)]

    def sides(x):
        if x.ndim == 3 and x.shape[0] > halo:
            first, last = x[:halo], x[x.shape[0] - halo :]
            is_even = lax.rem(lax.axis_index("az"), 2) == 0
            to_even, to_odd = jnp.where(is_even, last, first), jnp.where(is_even, first, last)
        else:
            to_even = to_odd = x
        return lax.ppermute(to_even, "az", even_pairs), lax.ppermute(to_odd, "az", odd_pairs)

    image_own = image.reshape(2 * rows_own, cells)
    image_other = halves(image_own)
    piece = struct((2 * bins, cells), BF16)
    starts, perms, unperm, *echo_pieces = call(
        functools.partial(prep_body, parts, bank, cells),
        (
            struct((bank + 1,), jnp.int32),
            struct((parts, bins, bins), BF16),
            struct((bins, bins), BF16),
            *[struct((2 * bins + 16, cells), BF16)] * parts,
        ),
        [VMEM] * 3,
        [pltpu.VMEM((2 * bins, cells), F32)],
        flops=4 * rows_own * 2 * cells * bins,
        out_specs=(SMEM, *[VMEM] * (parts + 2)),
    )(
        filter_index.reshape(2 * parts, bins),
        echoes.reshape(2 * rows_own, echoes.shape[2]),
        slot_time.reshape(1, slot_time.shape[0]),
    )
    compressed = call(
        functools.partial(compress_body, parts),
        [piece] * parts,
        [VMEM] * 4,
        [pltpu.VMEM((2 * rows_own, cells), F32), pltpu.VMEM((2 * rows_own, 2 * cells), BF16)],
        flops=16 * rows_own * rows_own * cells,
    )(image_own, image_other, range_matrix, perms)
    own = share(compressed)
    echo_own = share(echo_pieces)
    forward_bands, adjoint_bands = pl.pallas_call(
        functools.partial(bands_body, cells),
        grid=(bank,),
        out_shape=(
            struct((bank, 2 * cells, span * cells), BF16),
            struct((bank, span * cells, 2 * cells), BF16),
        ),
        in_specs=[pl.BlockSpec((1, 2, taps), lambda i: (i, 0, 0))],
        out_specs=(
            pl.BlockSpec((1, 2 * cells, span * cells), lambda i: (i, 0, 0)),
            pl.BlockSpec((1, span * cells, 2 * cells), lambda i: (i, 0, 0)),
        ),
        cost_estimate=pl.CostEstimate(flops=10**9, bytes_accessed=10**7, transcendentals=0),
    )(filter_bank)
    pieces, names = [], []
    for number, x in enumerate(own):
        step = number
        even, odd = sides(x)
        pieces += [x, even, odd]
        names += [("own", step), ("even", step), ("odd", step)]
    filter_flops = bank * bins * parts * 2 * span * cells * 2 * cells
    blocks = pltpu.VMEM((parts + 2 * halo, 2 * bins, cells), BF16)
    sums = pltpu.VMEM((parts, 2 * bins, cells), F32)
    residual = call(
        functools.partial(forward_body, parts, halo, names),
        struct((parts, 2 * bins, cells), BF16),
        [SMEM] + [VMEM] * (len(pieces) + 1 + len(echo_own)),
        [blocks, sums],
        flops=filter_flops,
    )(starts, *pieces, forward_bands, *echo_own)
    even, odd = sides(residual)
    back = call(
        functools.partial(adjoint_body, parts, halo),
        [piece] * parts,
        [SMEM] + [VMEM] * 5,
        [blocks, sums],
        flops=filter_flops,
    )(starts, even, residual, odd, adjoint_bands, unperm)
    back_own = share(back)
    back_other = [halves(x) for x in back_own]
    first_col = (1 - half) * rows_own
    moved = halves(lax.dynamic_slice_in_dim(range_matrix, first_col, rows_own, 2))
    gradient = call(
        functools.partial(gradient_body, parts),
        struct((2 * rows_own, cells), F32),
        [VMEM] * (2 * len(back_own) + 2),
        [pltpu.VMEM((2 * cells, rows_own), F32)] * 2,
        flops=16 * rows_own * rows_own * cells,
    )(*back_own, *back_other, range_matrix, moved)
    return gradient.reshape(rows_own, 2, cells)


def solution(mesh):
    return jax.shard_map(
        on_device,
        mesh=mesh,
        in_specs=(
            P(("frames", "cplx"), None, ("az", "rg")),
            P(("frames", "cplx"), None, ("az", "rg")),
            P(("frames", "az", "rg")),
            P(None, "cplx", None),
            P(),
            P(),
        ),
        out_specs=P(("frames", "cplx"), None, ("az", "rg")),
        check_vma=False,
    )
```

```python
import functools

import jax
import jax.numpy as jnp
from jax import lax
from jax.experimental import pallas as pl
from jax.experimental.pallas import tpu as pltpu
from jax.sharding import PartitionSpec as P

GROUP = 32
F32 = jnp.float32
BF16 = jnp.bfloat16
VMEM = pl.BlockSpec(memory_space=pltpu.VMEM)
SMEM = pl.BlockSpec(memory_space=pltpu.SMEM)


def mm(a, b):
    return jnp.dot(a, b, preferred_element_type=F32)


def mm_nt(a, b):
    return lax.dot_general(a, b, (((1,), (1,)), ((), ())), preferred_element_type=F32)


def mm_tn(a, b):
    return lax.dot_general(a, b, (((0,), (0,)), ((), ())), preferred_element_type=F32)


def iota(shape, axis):
    return lax.broadcasted_iota(jnp.int32, shape, axis)


def column_of(row):
    size = row.shape[1]
    eye = iota((size, size), 0) == iota((size, size), 1)
    return jnp.sum(jnp.where(eye, jnp.broadcast_to(row, (size, size)), 0.0), axis=1, keepdims=True)


def part_of(count, step):
    return lax.axis_index("rg") ^ step if count == 2 else step


def call(body, out_shape, in_specs, scratch=(), flops=0, out_specs=None, limit=None):
    count = sum(x.size * x.dtype.itemsize for x in jax.tree.leaves(out_shape))
    return pl.pallas_call(
        body,
        out_shape=out_shape,
        in_specs=in_specs,
        out_specs=jax.tree.map(lambda _: VMEM, out_shape) if out_specs is None else out_specs,
        scratch_shapes=list(scratch),
        cost_estimate=pl.CostEstimate(flops=flops, bytes_accessed=count, transcendentals=0),
        compiler_params=pltpu.CompilerParams(vmem_limit_bytes=limit or 20 * 2**20),
    )


def rank_of(ids):
    bins = ids.shape[1]
    key = (ids * bins + iota((1, bins), 1)).astype(F32)
    return jnp.sum((column_of(key) < key).astype(F32), axis=0, keepdims=True)


def split_complex(tmp_ref, values):
    bins = values.shape[0] // 2
    tmp_ref[0 : 2 * bins, :] = values
    return jnp.concatenate(
        [tmp_ref[pl.ds(0, bins, stride=2), :], tmp_ref[pl.ds(1, bins, stride=2), :]], axis=1
    ).astype(BF16)


def times_image(matrix_ref, rows, columns, image):
    cells = image.shape[1] // 2
    from_real = mm(matrix_ref[0, rows, columns], image)
    from_imag = mm(matrix_ref[1, rows, columns], image)
    return jnp.concatenate(
        [from_real[:, :cells] - from_imag[:, cells:], from_real[:, cells:] + from_imag[:, :cells]],
        axis=1,
    )


def half_columns(rows_own, half):
    return pl.ds(pl.multiple_of(half * rows_own, rows_own), rows_own)


def prep_body(parts, bank, cell_count, index_any, time_any, echo_any, image_any, matrix_any, *rest):
    starts_ref, perm_ref, unperm_ref, matrix_ref, moved_ref, begun_ref = rest[:6]
    echo_out = rest[6 : 6 + parts]
    index_ref, time_ref, echo_ref, image_ref, tmp_ref, sems = rest[6 + parts :]
    bins = perm_ref.shape[1]
    rows_own = bins * parts
    rg = lax.axis_index("rg")
    owner = lax.axis_index("az") * parts + rg
    half = lax.axis_index("cplx")
    loads = [
        pltpu.make_async_copy(*pair, sems.at[number])
        for number, pair in enumerate(
            (
                (index_any, index_ref),
                (time_any, time_ref),
                (echo_any, echo_ref),
                (image_any, image_ref),
                (matrix_any, matrix_ref),
                (matrix_any.at[:, :, half_columns(rows_own, 1 - half)], moved_ref),
            )
        )
    ]
    for load in loads:
        load.start()
    loads[0].wait()
    ids_half = index_ref[:, half_columns(rows_own, half)]
    pieces = [ids_half[:, part * bins : (part + 1) * bins] for part in range(parts)]

    def ids_of(part):
        return functools.reduce(
            lambda total, number: jnp.where(part == number, pieces[number], total),
            range(1, parts),
            pieces[0],
        )

    for step in range(parts):
        rank = rank_of(ids_of(part_of(parts, step)))
        perm_ref[step] = (iota((bins, bins), 0).astype(F32) == rank).astype(BF16)
    ids = ids_of(rg)
    unperm_ref[...] = (column_of(rank_of(ids)) == iota((bins, bins), 1).astype(F32)).astype(BF16)
    for number in range(bank + 1):
        starts_ref[number] = jnp.sum((ids < number).astype(F32)).astype(jnp.int32)
    loads[1].wait()
    local = (time_ref[...] - owner * cell_count).astype(F32)
    slots = local.shape[1]
    hits = column_of(local) == iota((slots, cell_count), 1).astype(F32)
    place = hits.astype(BF16)
    occupied = jnp.sum(hits.astype(F32), axis=0, keepdims=True)
    loads[2].wait()
    for step in range(parts):
        part = part_of(parts, step)
        rows = echo_ref[pl.ds(pl.multiple_of(part * 2 * bins, 2 * bins), 2 * bins), :]
        moved = mm(perm_ref[step], split_complex(tmp_ref, mm(rows, place))).astype(BF16)
        echo_out[step][0:bins, :] = moved[:, :cell_count]
        echo_out[step][bins : 2 * bins, :] = moved[:, cell_count:]
        echo_out[step][2 * bins :, :] = jnp.broadcast_to(occupied, (16, cell_count)).astype(BF16)
    loads[3].wait()
    image = split_complex(tmp_ref, image_ref[...].astype(F32))
    loads[4].wait()
    begun_ref[...] = times_image(matrix_ref, slice(None), half_columns(rows_own, half), image)
    loads[5].wait()


def bands_body(seg, bank_ref, fwd_ref, adj_ref):
    bank, _, taps = bank_ref.shape
    count = taps // seg
    later = iota((seg, seg), 1) >= iota((seg, seg), 0)
    zero = jnp.zeros((seg, seg), F32)

    def one(number, carry):
        values = bank_ref[number].astype(F32)
        for part in range(2):
            turned = [zero]
            for block in range(count):
                row = values[part : part + 1, block * seg : (block + 1) * seg]
                turned.append(
                    pltpu.roll(jnp.broadcast_to(row, (seg, seg)), 0, 1, stride=1, stride_axis=0)
                )
            turned.append(zero)
            columns = slice(part * seg, (part + 1) * seg)
            for block in range(count + 1):
                tile = jnp.where(later, turned[block + 1], turned[block]).astype(BF16)
                fwd_ref[number, columns, block * seg : (block + 1) * seg] = tile
                adj_ref[number, (count - block) * seg : (count - block + 1) * seg, columns] = tile
        return carry

    lax.fori_loop(0, bank, one, 0)


def compress_body(parts, image_ref, matrix_ref, perm_ref, begun_ref, *rest):
    outs, tmp_ref = rest[:parts], rest[parts]
    half = lax.axis_index("cplx")
    rows_own, cells = begun_ref.shape[0], begun_ref.shape[1] // 2
    bins = rows_own // parts
    image = split_complex(tmp_ref, image_ref[...].astype(F32))
    for step in range(parts):
        rows = pl.ds(pl.multiple_of(part_of(parts, step) * bins, bins), bins)
        made = begun_ref[rows, :] + times_image(
            matrix_ref, rows, half_columns(rows_own, 1 - half), image
        )
        sent = mm(perm_ref[step], made.astype(BF16)).astype(BF16)
        outs[step][:bins, :] = sent[:, :cells]
        outs[step][bins:, :] = sent[:, cells:]


def fill_blocks(blocks_ref, pieces):
    for ref, at in pieces:
        if len(ref.shape) == 2:
            blocks_ref[at] = ref[...]
        else:
            for number in range(ref.shape[0]):
                blocks_ref[at + number] = ref[number]


def side_bases(parts, halo):
    even = lax.rem(lax.axis_index("az"), 2) == 0
    right = halo + parts
    return jnp.where(even, right, 0), jnp.where(even, 0, right)


def filter_groups(starts_ref, bank, bins, group, work):
    align = min(16, group)
    last = bins - group

    def tile(number, at):
        low, high = starts_ref[number], starts_ref[number + 1]
        first = lax.div(low, align) * align + at * group
        first = pl.multiple_of(jnp.minimum(first, last), align)
        slot = iota((group, 1), 0) + first
        work(number, first, (slot >= low) & (slot < high))

    for number in range(bank):
        tile(number, 0)
    for number in range(bank):
        low, high = starts_ref[number], starts_ref[number + 1]
        count = lax.div(high - lax.div(low, align) * align + (group - 1), group)

        def more(at, carry, number=number):
            tile(number, at)
            return carry

        lax.fori_loop(1, count, more, 0)


def windows(blocks_ref, parts, first, group, bins, span):
    loaded = [
        [blocks_ref[block, pl.ds(side * bins + first, group), :] for block in range(blocks_ref.shape[0])]
        for side in range(2)
    ]
    return jnp.concatenate(
        [
            jnp.concatenate(loaded[side][block : block + span], axis=1)
            for block in range(parts)
            for side in range(2)
        ],
        axis=0,
    )


def forward_body(parts, halo, names, starts_ref, *rest):
    count = len(names)
    pieces, bands_ref = rest[:count], rest[count]
    echoes = rest[count + 1 : -3]
    out_ref, blocks_ref, sum_ref = rest[-3:]
    bank, cells = bands_ref.shape[0], blocks_ref.shape[2]
    bins = blocks_ref.shape[1] // 2
    span = bands_ref.shape[2] // cells
    group = min(GROUP, bins)
    even_base, odd_base = side_bases(parts, halo)
    base = {"even": even_base, "odd": odd_base, "own": halo}
    fill_blocks(blocks_ref, [(ref, base[side] + (part_of(parts, step) if parts == 2 else step)) for ref, (side, step) in zip(pieces, names)])

    def work(number, first, mask):
        made = mm_nt(windows(blocks_ref, parts, first, group, bins, span), bands_ref[number])
        for block in range(parts):
            top = made[2 * block * group : (2 * block + 1) * group]
            low = made[(2 * block + 1) * group : (2 * block + 2) * group]
            for side, value in enumerate((top[:, :cells] - low[:, cells:], top[:, cells:] + low[:, :cells])):
                rows = pl.ds(side * bins + first, group)
                sum_ref[block, rows, :] = jnp.where(mask, value, sum_ref[block, rows, :])

    filter_groups(starts_ref, bank, bins, group, work)
    for step in range(parts):
        part = part_of(parts, step)
        echo = echoes[step][...] if len(echoes) > 1 else echoes[0][step]
        occupied = echo[2 * bins : 2 * bins + 1].astype(F32)
        model = sum_ref[part].astype(BF16).astype(F32)
        out_ref[part] = (occupied * model - echo[: 2 * bins].astype(F32)).astype(BF16)


def adjoint_body(parts, halo, starts_ref, even_ref, own_ref, odd_ref, bands_ref, perm_ref, *rest):
    outs, (blocks_ref, sum_ref) = rest[:parts], rest[parts:]
    bank, cells = bands_ref.shape[0], blocks_ref.shape[2]
    bins = blocks_ref.shape[1] // 2
    span = bands_ref.shape[1] // cells
    group = min(GROUP, bins)
    even_base, odd_base = side_bases(parts, halo)
    fill_blocks(blocks_ref, [(even_ref, even_base), (own_ref, halo), (odd_ref, odd_base)])

    def work(number, first, mask):
        made = mm(windows(blocks_ref, parts, first, group, bins, span), bands_ref[number])
        for block in range(parts):
            top = made[2 * block * group : (2 * block + 1) * group]
            low = made[(2 * block + 1) * group : (2 * block + 2) * group]
            for side, value in enumerate((top[:, :cells] + low[:, cells:], low[:, :cells] - top[:, cells:])):
                rows = pl.ds(side * bins + first, group)
                sum_ref[block, rows, :] = jnp.where(mask, value, sum_ref[block, rows, :])

    filter_groups(starts_ref, bank, bins, group, work)
    for step in range(parts):
        part = part_of(parts, step)
        both = jnp.concatenate([sum_ref[part, :bins, :], sum_ref[part, bins:, :]], axis=1).astype(BF16)
        both = mm(perm_ref[...], both).astype(BF16)
        outs[step][:bins, :] = both[:, :cells]
        outs[step][bins:, :] = both[:, cells:]


def gradient_body(parts, mine, steps, begun, final, *refs):
    pieces, refs = refs[: len(steps)], refs[len(steps) :]
    matrix_ref, refs = refs[0], refs[1:]
    begun_ref, refs = (refs[0], refs[1:]) if begun else (None, refs)
    out_ref = refs[0]
    rows_own = matrix_ref.shape[1]
    cells = pieces[0].shape[-1]
    bins = rows_own // parts
    columns = half_columns(rows_own, lax.axis_index("cplx")) if mine else slice(None)
    total = (begun_ref[0], begun_ref[1]) if begun else None
    for ref, step in zip(pieces, steps):
        for number in range(1 if len(ref.shape) == 2 else ref.shape[0]):
            piece = ref[...] if len(ref.shape) == 2 else ref[number]
            part = part_of(parts, step) if len(ref.shape) == 2 else number
            both = jnp.concatenate([piece[:bins], piece[bins:]], axis=1)
            rows = pl.ds(pl.multiple_of(part * bins, bins), bins)
            made = [mm_tn(both, matrix_ref[side, rows, columns]) for side in range(2)]
            total = made if total is None else [x + y for x, y in zip(total, made)]
    if not final:
        out_ref[0], out_ref[1] = total
        return
    real, imag = total
    out_ref[pl.ds(0, rows_own, stride=2), :] = (real[:cells, :] + imag[cells:, :]).T
    out_ref[pl.ds(1, rows_own, stride=2), :] = (real[cells:, :] - imag[:cells, :]).T


def swap_pairs(count, first):
    pairs = []
    for low in range(first, count - 1, 2):
        pairs += [(low, low + 1), (low + 1, low)]
    return pairs


def on_device(image, echoes, slot_time, range_matrix, filter_bank, filter_index):
    rows_own, _, cells = image.shape
    parts, rows_az = lax.axis_size("rg"), lax.axis_size("az")
    bins = rows_own // parts
    bank, _, taps = filter_bank.shape
    halo = taps // 2 // cells
    span = taps // cells + 1
    flip = [(0, 1), (1, 0)]
    struct = jax.ShapeDtypeStruct
    even_pairs, odd_pairs = swap_pairs(rows_az, 0), swap_pairs(rows_az, 1)

    def halves(x):
        return lax.ppermute(x, "cplx", flip)

    def share(pieces):
        if parts == 2:
            return [pieces[0], lax.ppermute(pieces[1], "rg", flip)]
        return [lax.all_to_all(jnp.stack(pieces), "rg", split_axis=0, concat_axis=0)]

    def sides(x):
        if x.ndim == 3 and x.shape[0] > halo:
            first, last = x[:halo], x[x.shape[0] - halo :]
            is_even = lax.rem(lax.axis_index("az"), 2) == 0
            to_even, to_odd = jnp.where(is_even, last, first), jnp.where(is_even, first, last)
        else:
            to_even = to_odd = x
        even = lax.ppermute(to_even, "az", even_pairs)
        odd = lax.ppermute(to_odd, "az", odd_pairs)
        return even, odd

    image_own = image.reshape(2 * rows_own, cells)
    image_other = halves(image_own)
    piece = struct((2 * bins, cells), BF16)
    starts, perms, unperm, matrix, moved, begun, *echo_pieces = call(
        functools.partial(prep_body, parts, bank, cells),
        (
            struct((bank + 1,), jnp.int32),
            struct((parts, bins, bins), BF16),
            struct((bins, bins), BF16),
            struct(range_matrix.shape, BF16),
            struct((2, rows_own, rows_own), BF16),
            struct((rows_own, 2 * cells), F32),
            *[struct((2 * bins + 16, cells), BF16)] * parts,
        ),
        [pl.BlockSpec(memory_space=pltpu.HBM)] * 5,
        [
            pltpu.VMEM((1, filter_index.shape[0]), jnp.int32),
            pltpu.VMEM((1, slot_time.shape[0]), jnp.int32),
            pltpu.VMEM((2 * rows_own, echoes.shape[2]), BF16),
            pltpu.VMEM((2 * rows_own, cells), BF16),
            pltpu.VMEM((2 * rows_own, cells), F32),
            pltpu.SemaphoreType.DMA((6,)),
        ],
        flops=8 * rows_own * rows_own * cells,
        out_specs=(SMEM, *[VMEM] * (parts + 5)),
    )(
        *[
            pltpu.with_memory_space_constraint(x, pltpu.HBM)
            for x in (
                filter_index.reshape(1, filter_index.shape[0]),
                slot_time.reshape(1, slot_time.shape[0]),
                echoes.reshape(2 * rows_own, echoes.shape[2]),
                image_own,
                range_matrix,
            )
        ]
    )
    compressed = call(
        functools.partial(compress_body, parts),
        [piece] * parts,
        [VMEM] * 4,
        [pltpu.VMEM((2 * rows_own, cells), F32)],
        flops=8 * rows_own * rows_own * cells,
    )(image_other, matrix, perms, begun)
    own = share(compressed)
    pieces, names = [], []
    for step, x in enumerate(own):
        even, odd = sides(x)
        pieces += [x, even, odd]
        names += [("own", step), ("even", step), ("odd", step)]
    echo_own = share(echo_pieces)
    moved = halves(moved)
    forward_bands, adjoint_bands = call(
        functools.partial(bands_body, cells),
        (
            struct((bank, 2 * cells, span * cells), BF16),
            struct((bank, span * cells, 2 * cells), BF16),
        ),
        [VMEM],
        flops=10**9,
    )(filter_bank)
    filter_flops = 2 * bins * parts * 2 * span * cells * 2 * cells
    blocks = pltpu.VMEM((parts + 2 * halo, 2 * bins, cells), BF16)
    sums = pltpu.VMEM((parts, 2 * bins, cells), F32)
    residual = call(
        functools.partial(forward_body, parts, halo, names),
        struct((parts, 2 * bins, cells), BF16),
        [SMEM] + [VMEM] * (len(pieces) + 1 + len(echo_own)),
        [blocks, sums],
        flops=filter_flops,
    )(starts, *pieces, forward_bands, *echo_own)
    even, odd = sides(residual)
    back = call(
        functools.partial(adjoint_body, parts, halo),
        [piece] * parts,
        [SMEM] + [VMEM] * 5,
        [blocks, sums],
        flops=filter_flops,
    )(starts, even, residual, odd, adjoint_bands, unperm)

    def project(pieces, steps, mine, begun=None, final=False):
        out = struct((2 * rows_own, cells), F32) if final else struct((2, 2 * cells, rows_own), F32)
        args = [*pieces, matrix if mine else moved] + ([] if begun is None else [begun])
        return call(
            functools.partial(gradient_body, parts, mine, steps, begun is not None, final),
            out,
            [VMEM] * len(args),
            flops=8 * len(pieces) * rows_own * bins * 2 * cells,
        )(*args)

    back_own = share(back)
    back_other = []
    for x in back_own:
        back_other.append(halves(x))
    total = None
    for number in range(len(back_own)):
        last = number == len(back_own) - 1
        total = project([back_own[number]], [number], True, total)
        total = project([back_other[number]], [number], False, total, last)
    return total.reshape(rows_own, 2, cells)


def solution(mesh):
    return jax.shard_map(
        on_device,
        mesh=mesh,
        in_specs=(
            P(("frames", "cplx"), None, ("az", "rg")),
            P(("frames", "cplx"), None, ("az", "rg")),
            P(("frames", "az", "rg")),
            P(None, "cplx", None),
            P(),
            P(),
        ),
        out_specs=P(("frames", "cplx"), None, ("az", "rg")),
        check_vma=False,
    )
```

```python
import functools

import jax
import jax.numpy as jnp
from jax import lax
from jax.experimental import pallas as pl
from jax.experimental.pallas import tpu as pltpu
from jax.sharding import PartitionSpec as P

GROUP = 48
ALIGN = 16
UNROLL = 3
F32 = jnp.float32
BF16 = jnp.bfloat16
VMEM = pl.BlockSpec(memory_space=pltpu.VMEM)
SMEM = pl.BlockSpec(memory_space=pltpu.SMEM)


def mm(a, b):
    return jnp.dot(a, b, preferred_element_type=F32)


def iota(shape, axis):
    return lax.broadcasted_iota(jnp.int32, shape, axis)


def column_of(row):
    size = row.shape[1]
    eye = iota((size, size), 0) == iota((size, size), 1)
    return jnp.sum(jnp.where(eye, jnp.broadcast_to(row, (size, size)), 0.0), axis=1, keepdims=True)


def part_of(count, step):
    return lax.axis_index("rg") ^ step if count == 2 else step


def call(body, out_shape, in_specs, scratch=(), flops=0, out_specs=None, limit=None):
    count = sum(x.size * x.dtype.itemsize for x in jax.tree.leaves(out_shape))
    return pl.pallas_call(
        body,
        out_shape=out_shape,
        in_specs=in_specs,
        out_specs=jax.tree.map(lambda _: VMEM, out_shape) if out_specs is None else out_specs,
        scratch_shapes=list(scratch),
        cost_estimate=pl.CostEstimate(flops=flops, bytes_accessed=count, transcendentals=0),
        compiler_params=pltpu.CompilerParams(vmem_limit_bytes=limit or 20 * 2**20),
    )


def rank_of(ids):
    bins = ids.shape[1]
    key = (ids * bins + iota((1, bins), 1)).astype(F32)
    return jnp.sum((column_of(key) < key).astype(F32), axis=0, keepdims=True)


def split_complex(tmp_ref, values):
    bins = values.shape[0] // 2
    tmp_ref[0 : 2 * bins, :] = values
    return jnp.concatenate(
        [tmp_ref[pl.ds(0, bins, stride=2), :], tmp_ref[pl.ds(1, bins, stride=2), :]], axis=1
    ).astype(BF16)


def times_image(matrix_ref, rows, columns, image):
    cells = image.shape[1] // 2
    from_real = mm(matrix_ref[0, rows, columns], image)
    from_imag = mm(matrix_ref[1, rows, columns], image)
    return jnp.concatenate(
        [from_real[:, :cells] - from_imag[:, cells:], from_real[:, cells:] + from_imag[:, :cells]],
        axis=1,
    )


def half_columns(rows_own, half):
    return pl.ds(pl.multiple_of(half * rows_own, rows_own), rows_own)


def prep_body(parts, index_any, image_any, matrix_any, *rest):
    perm_ref, matrix_ref, begun_ref, index_ref, image_ref, tmp_ref, sems = rest
    bins, rows_own = perm_ref.shape[1:]
    half = lax.axis_index("cplx")
    loads = [
        pltpu.make_async_copy(*pair, sems.at[number])
        for number, pair in enumerate(
            ((index_any, index_ref), (image_any, image_ref), (matrix_any, matrix_ref))
        )
    ]
    for load in loads:
        load.start()
    loads[0].wait()
    rank = rank_of(index_ref[:, half_columns(rows_own, half)])
    for step in range(parts):
        slot = (iota((bins, 1), 0) + part_of(parts, step) * bins).astype(F32)
        perm_ref[step] = (slot == rank).astype(BF16)
    loads[1].wait()
    image = split_complex(tmp_ref, image_ref[...].astype(F32))
    loads[2].wait()
    begun_ref[...] = times_image(matrix_ref, slice(None), half_columns(rows_own, half), image)


def make_bands(seg, starts_ref, table_ref, bands_ref):
    count = table_ref.shape[1] // seg
    later = iota((seg, seg), 1) >= iota((seg, seg), 0)

    def one(number):
        for part in range(2):
            row = table_ref[pl.ds(2 * number + part, 1), :]
            before = jnp.zeros((seg, seg), F32)
            columns = slice(part * seg, (part + 1) * seg)
            for block in range(count):
                same = jnp.broadcast_to(row[:, block * seg : (block + 1) * seg], (seg, seg))
                turned = pltpu.roll(same, 0, 1, stride=1, stride_axis=0)
                tile = jnp.where(later, turned, before).astype(BF16)
                bands_ref[number, (count - 1 - block) * seg : (count - block) * seg, columns] = tile
                before = turned

    def one_used(number, carry):
        pl.when(starts_ref[number + 1] > starts_ref[number])(lambda: one(number))
        return carry

    lax.fori_loop(0, bands_ref.shape[0], one_used, 0)


def fill_table(bank_ref, table_ref):
    bank, _, taps = bank_ref.shape
    table_ref[:, taps:] = jnp.zeros((2 * bank, table_ref.shape[1] - taps), F32)
    for number in range(bank):
        table_ref[2 * number : 2 * number + 2, :taps] = bank_ref[number].astype(F32)


def adjoint_bands_body(seg, starts_ref, bank_ref, bands_ref, table_ref):
    fill_table(bank_ref, table_ref)
    make_bands(seg, starts_ref, table_ref, bands_ref)


def list_tiles(ids, group, starts_ref, number_ref, first_ref):
    bank, bins = starts_ref.shape[0] - 2, ids.shape[1] // lax.axis_size("rg")
    base = lax.axis_index("rg") * bins
    for number in range(bank + 1):
        before = jnp.sum((ids < number).astype(F32)).astype(jnp.int32)
        starts_ref[number] = jnp.clip(before - base, 0, bins)

    def per_filter(number, count):
        low, high = starts_ref[number], starts_ref[number + 1]
        aligned = lax.div(low, ALIGN) * ALIGN

        def per_tile(at, count):
            number_ref[count] = number
            first_ref[count] = jnp.minimum(aligned + at * group, bins - group)
            return count + 1

        tiles = jnp.where(high > low, lax.div(high - aligned + (group - 1), group), 0)
        return lax.fori_loop(0, tiles, per_tile, count)

    count = lax.fori_loop(0, bank, per_filter, 0)
    starts_ref[bank + 1] = count
    for extra in range(UNROLL - 1):
        number_ref[count + extra] = number_ref[count - 1]
        first_ref[count + extra] = first_ref[count - 1]


def bands_body(cell_count, group, index_ref, bank_ref, *rest):
    starts_ref, number_ref, first_ref, bands_ref, table_ref = rest
    _, _, taps = bank_ref.shape
    rows_own = index_ref.shape[1] // lax.axis_size("cplx")
    ids = index_ref[:, half_columns(rows_own, lax.axis_index("cplx"))]
    list_tiles(ids, group, starts_ref, number_ref, first_ref)
    fill_table(bank_ref, table_ref)
    width = table_ref.shape[1]
    turn = (iota((taps, width), 0) + iota((taps, width), 1) == taps).astype(BF16)
    table_ref[...] = mm(table_ref[:, :taps].astype(BF16), turn)
    make_bands(cell_count, starts_ref, table_ref, bands_ref)


def echo_body(parts, cell_count, time_any, echo_any, perm_ref, *rest):
    outs, (time_ref, echo_ref, tmp_ref, sems) = rest[:parts], rest[parts:]
    bins = perm_ref.shape[1]
    owner = lax.axis_index("az") * parts + lax.axis_index("rg")
    loads = [
        pltpu.make_async_copy(time_any, time_ref, sems.at[0]),
        pltpu.make_async_copy(echo_any, echo_ref, sems.at[1]),
    ]
    for load in loads:
        load.start()
    loads[0].wait()
    local = (time_ref[...] - owner * cell_count).astype(F32)
    slots = local.shape[1]
    hits = column_of(local) == iota((slots, cell_count), 1).astype(F32)
    place = hits.astype(BF16)
    occupied = jnp.sum(hits.astype(F32), axis=0, keepdims=True)
    loads[1].wait()
    gridded = split_complex(tmp_ref, mm(echo_ref[...], place))
    for step in range(parts):
        moved = mm(perm_ref[step], gridded).astype(BF16)
        outs[step][0:bins, :] = moved[:, :cell_count]
        outs[step][bins : 2 * bins, :] = moved[:, cell_count:]
        outs[step][2 * bins :, :] = jnp.broadcast_to(occupied, (16, cell_count)).astype(BF16)


def compress_body(step, image_ref, matrix_ref, perm_ref, begun_ref, out_ref, made_ref, tmp_ref):
    rows_own = begun_ref.shape[0]
    image = split_complex(tmp_ref, image_ref[...].astype(F32))
    columns = half_columns(rows_own, 1 - lax.axis_index("cplx"))
    made_ref[...] = (begun_ref[...] + times_image(matrix_ref, slice(None), columns, image)).astype(BF16)
    sort_body(step, made_ref, perm_ref, out_ref)


def sort_body(step, made_ref, perm_ref, out_ref):
    bins, cells = perm_ref.shape[1], made_ref.shape[1] // 2
    sent = mm(perm_ref[step], made_ref[...]).astype(BF16)
    out_ref[:bins, :] = sent[:, :cells]
    out_ref[bins:, :] = sent[:, cells:]


def sorted_matrix(parts, matrix_ref, perm_ref, columns, store):
    bins = perm_ref.shape[1]
    for step in range(parts):
        rows = pl.ds(pl.multiple_of(part_of(parts, step) * bins, bins), bins)
        for side in range(2):
            store(side, rows, mm(perm_ref[step], matrix_ref[side, :, columns]).astype(BF16))


def sort_sent_body(parts, matrix_ref, perm_ref, out_ref):
    def store(side, rows, value):
        out_ref[side, rows, :] = value

    columns = half_columns(matrix_ref.shape[1], 1 - lax.axis_index("cplx"))
    sorted_matrix(parts, matrix_ref, perm_ref, columns, store)


def fill_blocks(blocks_ref, pieces):
    for ref, at in pieces:
        if len(ref.shape) == 2:
            blocks_ref[at] = ref[...]
        else:
            for number in range(ref.shape[0]):
                blocks_ref[at + number] = ref[number]


def side_bases(parts, halo):
    even = lax.rem(lax.axis_index("az"), 2) == 0
    right = halo + parts
    return jnp.where(even, right, 0), jnp.where(even, 0, right)


def filter_groups(starts_ref, number_ref, first_ref, group, work):
    def run(chunk, carry):
        for at in range(UNROLL):
            number = number_ref[chunk * UNROLL + at]
            first = pl.multiple_of(first_ref[chunk * UNROLL + at], ALIGN)
            slot = iota((group, 1), 0) + first
            work(number, first, (slot >= starts_ref[number]) & (slot < starts_ref[number + 1]))
        return carry

    count = starts_ref[starts_ref.shape[0] - 1]
    lax.fori_loop(0, lax.div(count + (UNROLL - 1), UNROLL), run, 0)


def filtered(blocks_ref, bands, outputs, first, group, sign):
    cells, bins = blocks_ref.shape[2], blocks_ref.shape[1] // 2
    span = bands.shape[0] // cells
    rows = [
        jnp.concatenate(
            [blocks_ref[block + at, pl.ds(side * bins + first, group), :] for at in range(span)], axis=1
        )
        for block in outputs
        for side in range(2)
    ]
    made = mm(jnp.concatenate(rows, axis=0), bands)
    results = []
    for number in range(len(outputs)):
        top = made[2 * number * group : (2 * number + 1) * group]
        low = made[(2 * number + 1) * group : (2 * number + 2) * group]
        results.append(
            (top[:, :cells] - sign * low[:, cells:], low[:, :cells] + sign * top[:, cells:])
        )
    return results


def filter_all(parts, group, tiles, blocks_ref, bands_ref, sum_ref, sign):
    bins = blocks_ref.shape[1] // 2

    def work(number, first, mask):
        made = filtered(blocks_ref, bands_ref[number], range(parts), first, group, sign)
        for block in range(parts):
            for side in range(2):
                rows = pl.ds(side * bins + first, group)
                sum_ref[block, rows, :] = jnp.where(mask, made[block][side], sum_ref[block, rows, :])

    filter_groups(*tiles, group, work)


def forward_body(parts, halo, group, names, *refs):
    tiles, rest = refs[:3], refs[3:]
    count = len(names)
    pieces, bands_ref = rest[:count], rest[count]
    echoes = rest[count + 1 : -3]
    out_ref, blocks_ref, sum_ref = rest[-3:]
    bins = blocks_ref.shape[1] // 2
    even_base, odd_base = side_bases(parts, halo)
    base = {"even": even_base, "odd": odd_base, "own": halo}
    fill_blocks(
        blocks_ref,
        [
            (ref, base[side] + (part_of(parts, step) if parts == 2 else step))
            for ref, (side, step) in zip(pieces, names)
        ],
    )
    filter_all(parts, group, tiles, blocks_ref, bands_ref, sum_ref, 1.0)
    for step in range(parts):
        part = part_of(parts, step)
        echo = echoes[step][...] if len(echoes) > 1 else echoes[0][step]
        occupied = echo[2 * bins : 2 * bins + 1].astype(F32)
        model = sum_ref[part].astype(BF16).astype(F32)
        out_ref[part] = (occupied * model - echo[: 2 * bins].astype(F32)).astype(BF16)


def adjoint_body(parts, halo, group, *refs):
    tiles, (even_ref, own_ref, odd_ref, bands_ref) = refs[:3], refs[3:7]
    outs, (blocks_ref, sum_ref) = refs[7 : 7 + parts], refs[7 + parts :]
    even_base, odd_base = side_bases(parts, halo)
    fill_blocks(blocks_ref, [(even_ref, even_base), (own_ref, halo), (odd_ref, odd_base)])
    filter_all(parts, group, tiles, blocks_ref, bands_ref, sum_ref, -1.0)
    for step in range(parts):
        outs[step][...] = sum_ref[part_of(parts, step)].astype(BF16)


def turn_body(parts, matrix_ref, perm_ref, moved_ref, out_ref, sorted_ref):
    def store(side, rows, value):
        sorted_ref[side, rows, :] = value

    columns = half_columns(matrix_ref.shape[1], lax.axis_index("cplx"))
    sorted_matrix(parts, matrix_ref, perm_ref, columns, store)
    for side in range(2):
        out_ref[0, side] = sorted_ref[side].T
        out_ref[1, side] = moved_ref[side].T


def gradient_body(parts, source, step, begun, final, piece_ref, turned_ref, *refs):
    out_ref = refs[-1]
    rows_own = turned_ref.shape[2]
    cells = piece_ref.shape[-1]
    bins = rows_own // parts
    pieces = [piece_ref[...]] if len(piece_ref.shape) == 2 else [piece_ref[n] for n in range(parts)]
    both = jnp.concatenate(
        [jnp.concatenate([x[:bins], x[bins:]], axis=1) for x in pieces], axis=0
    )
    if len(pieces) > 1:
        columns = slice(None)
    else:
        columns = pl.ds(pl.multiple_of(part_of(parts, step) * bins, bins), bins)
    real, imag = [mm(turned_ref[source, side, :, columns], both) for side in range(2)]
    total = [real[:, :cells] + imag[:, cells:], real[:, cells:] - imag[:, :cells]]
    if begun:
        total = [total[0] + refs[0][:, :cells], total[1] + refs[0][:, cells:]]
    if final:
        out_ref[pl.ds(0, rows_own, stride=2), :] = total[0]
        out_ref[pl.ds(1, rows_own, stride=2), :] = total[1]
    else:
        out_ref[:, :cells] = total[0]
        out_ref[:, cells:] = total[1]


def swap_pairs(count, first):
    pairs = []
    for low in range(first, count - 1, 2):
        pairs += [(low, low + 1), (low + 1, low)]
    return pairs


def on_device(image, echoes, slot_time, range_matrix, filter_bank, filter_index):
    rows_own, _, cells = image.shape
    parts, rows_az = lax.axis_size("rg"), lax.axis_size("az")
    bins = rows_own // parts
    bank, _, taps = filter_bank.shape
    halo = taps // 2 // cells
    span = taps // cells + 1
    flip = [(0, 1), (1, 0)]
    struct = jax.ShapeDtypeStruct
    even_pairs, odd_pairs = swap_pairs(rows_az, 0), swap_pairs(rows_az, 1)

    def halves(x):
        return lax.ppermute(x, "cplx", flip)

    def share(pieces):
        if parts == 2:
            return [pieces[0], lax.ppermute(pieces[1], "rg", flip)]
        return [lax.all_to_all(jnp.stack(pieces), "rg", split_axis=0, concat_axis=0)]

    def sides(x):
        if x.ndim == 3 and x.shape[0] > halo:
            first, last = x[:halo], x[x.shape[0] - halo :]
            is_even = lax.rem(lax.axis_index("az"), 2) == 0
            to_even, to_odd = jnp.where(is_even, last, first), jnp.where(is_even, first, last)
        else:
            to_even = to_odd = x
        even = lax.ppermute(to_even, "az", even_pairs)
        odd = lax.ppermute(to_odd, "az", odd_pairs)
        return even, odd

    image_own = image.reshape(2 * rows_own, cells)
    image_other = halves(image_own)
    piece = struct((2 * bins, cells), BF16)
    in_hbm = pl.BlockSpec(memory_space=pltpu.HBM)

    def stay(*arrays):
        return [pltpu.with_memory_space_constraint(x, pltpu.HBM) for x in arrays]

    index_row = filter_index.reshape(1, filter_index.shape[0])
    split_space = pltpu.VMEM((2 * rows_own, cells), F32)
    perms, matrix, begun = call(
        functools.partial(prep_body, parts),
        (
            struct((parts, bins, rows_own), BF16),
            struct(range_matrix.shape, BF16),
            struct((rows_own, 2 * cells), F32),
        ),
        [in_hbm] * 3,
        [
            pltpu.VMEM(index_row.shape, jnp.int32),
            pltpu.VMEM((2 * rows_own, cells), BF16),
            split_space,
            pltpu.SemaphoreType.DMA((3,)),
        ],
        flops=8 * rows_own * rows_own * cells,
    )(*stay(index_row, image_own, range_matrix))
    compressed = [None] * parts
    last = parts - 1
    compressed[last], made = call(
        functools.partial(compress_body, last),
        (piece, struct((rows_own, 2 * cells), BF16)),
        [VMEM] * 4,
        [split_space],
        flops=8 * rows_own * rows_own * cells,
    )(image_other, matrix, perms, begun)
    for step in range(last):
        compressed[step] = call(
            functools.partial(sort_body, step), piece, [VMEM] * 2, flops=4 * rows_own * bins * cells
        )(made, perms)
    own = share(compressed)
    echo_pieces = call(
        functools.partial(echo_body, parts, cells),
        [struct((2 * bins + 16, cells), BF16)] * parts,
        [in_hbm] * 2 + [VMEM],
        [
            pltpu.VMEM((1, slot_time.shape[0]), jnp.int32),
            pltpu.VMEM((2 * rows_own, echoes.shape[2]), BF16),
            split_space,
            pltpu.SemaphoreType.DMA((2,)),
        ],
        flops=4 * rows_own * rows_own * cells,
    )(
        *stay(
            slot_time.reshape(1, slot_time.shape[0]),
            echoes.reshape(2 * rows_own, echoes.shape[2]),
        ),
        perms,
    )
    echo_own = share(echo_pieces)
    pieces, names = [], []
    for step, x in enumerate(own):
        even, odd = sides(x)
        pieces += [x, even, odd]
        names += [("own", step), ("even", step), ("odd", step)]
    group = min(GROUP, bins)
    tile_count = bins // group + 2 * bank + UNROLL
    table_space = pltpu.VMEM((2 * bank, span * cells), F32)
    bands_struct = struct((bank, span * cells, 2 * cells), BF16)
    *tiles, forward_bands = call(
        functools.partial(bands_body, cells, group),
        (
            struct((bank + 2,), jnp.int32),
            struct((tile_count,), jnp.int32),
            struct((tile_count,), jnp.int32),
            bands_struct,
        ),
        [VMEM] * 2,
        [table_space],
        flops=10**9,
        out_specs=(SMEM, SMEM, SMEM, VMEM),
    )(index_row, filter_bank)
    moved = call(
        functools.partial(sort_sent_body, parts),
        struct((2, rows_own, rows_own), BF16),
        [VMEM] * 2,
        flops=4 * rows_own**3,
    )(matrix, perms)
    moved = halves(moved)
    filter_flops = 2 * bins * parts * 2 * span * cells * 2 * cells
    spaces = [
        pltpu.VMEM((parts + 2 * halo, 2 * bins, cells), BF16),
        pltpu.VMEM((parts, 2 * bins, cells), F32),
    ]
    residual = call(
        functools.partial(forward_body, parts, halo, group, names),
        struct((parts, 2 * bins, cells), BF16),
        [SMEM] * 3 + [VMEM] * (len(pieces) + 1 + len(echo_own)),
        spaces,
        flops=filter_flops,
    )(*tiles, *pieces, forward_bands, *echo_own)
    even, odd = sides(residual)
    adjoint_bands = call(
        functools.partial(adjoint_bands_body, cells),
        bands_struct,
        [SMEM, VMEM],
        [table_space],
        flops=10**9,
    )(tiles[0], filter_bank)
    turned = call(
        functools.partial(turn_body, parts),
        struct((2, 2, rows_own, rows_own), BF16),
        [VMEM] * 3,
        [pltpu.VMEM((2, rows_own, rows_own), BF16)],
        flops=4 * rows_own**3,
    )(matrix, perms, moved)
    back = call(
        functools.partial(adjoint_body, parts, halo, group),
        [piece] * parts,
        [SMEM] * 3 + [VMEM] * 4,
        spaces,
        flops=filter_flops,
    )(*tiles, even, residual, odd, adjoint_bands)
    back_own = share(back)
    back_other = []
    for x in back_own:
        back_other.append(halves(x))
    total = None
    for number in range(len(back_own)):
        for source, x in enumerate((back_own[number], back_other[number])):
            final = source == 1 and number == len(back_own) - 1
            args = [x, turned] + ([] if total is None else [total])
            total = call(
                functools.partial(gradient_body, parts, source, number, total is not None, final),
                struct((2 * rows_own, cells) if final else (rows_own, 2 * cells), F32),
                [VMEM] * len(args),
                flops=8 * rows_own * bins * 2 * cells,
            )(*args)
    return total.reshape(rows_own, 2, cells)


def solution(mesh):
    return jax.shard_map(
        on_device,
        mesh=mesh,
        in_specs=(
            P(("frames", "cplx"), None, ("az", "rg")),
            P(("frames", "cplx"), None, ("az", "rg")),
            P(("frames", "az", "rg")),
            P(None, "cplx", None),
            P(),
            P(),
        ),
        out_specs=P(("frames", "cplx"), None, ("az", "rg")),
        check_vma=False,
    )
```

```python
import functools

import jax
import jax.numpy as jnp
from jax import lax
from jax.experimental import pallas as pl
from jax.experimental.pallas import tpu as pltpu
from jax.sharding import PartitionSpec as P

GROUP = 48
ALIGN = 16
UNROLL = 3
F32 = jnp.float32
BF16 = jnp.bfloat16
VMEM = pl.BlockSpec(memory_space=pltpu.VMEM)
SMEM = pl.BlockSpec(memory_space=pltpu.SMEM)


def mm(a, b):
    return jnp.dot(a, b, preferred_element_type=F32)


def iota(shape, axis):
    return lax.broadcasted_iota(jnp.int32, shape, axis)


def column_of(row):
    size = row.shape[1]
    eye = iota((size, size), 0) == iota((size, size), 1)
    return jnp.sum(jnp.where(eye, jnp.broadcast_to(row, (size, size)), 0.0), axis=1, keepdims=True)


def part_of(count, step):
    return lax.axis_index("rg") ^ step if count == 2 else step


def call(body, out_shape, in_specs, scratch=(), flops=0, out_specs=None, limit=None):
    count = sum(x.size * x.dtype.itemsize for x in jax.tree.leaves(out_shape))
    return pl.pallas_call(
        body,
        out_shape=out_shape,
        in_specs=in_specs,
        out_specs=jax.tree.map(lambda _: VMEM, out_shape) if out_specs is None else out_specs,
        scratch_shapes=list(scratch),
        cost_estimate=pl.CostEstimate(flops=flops, bytes_accessed=count, transcendentals=0),
        compiler_params=pltpu.CompilerParams(vmem_limit_bytes=limit or 20 * 2**20),
    )


def rank_of(ids):
    bins = ids.shape[1]
    key = (ids * bins + iota((1, bins), 1)).astype(F32)
    return jnp.sum((column_of(key) < key).astype(F32), axis=0, keepdims=True)


def split_complex(tmp_ref, values):
    bins = values.shape[0] // 2
    tmp_ref[0 : 2 * bins, :] = values
    return jnp.concatenate(
        [tmp_ref[pl.ds(0, bins, stride=2), :], tmp_ref[pl.ds(1, bins, stride=2), :]], axis=1
    ).astype(BF16)


def times_image(matrix_ref, rows, columns, image):
    cells = image.shape[1] // 2
    from_real = mm(matrix_ref[0, rows, columns], image)
    from_imag = mm(matrix_ref[1, rows, columns], image)
    return jnp.concatenate(
        [from_real[:, :cells] - from_imag[:, cells:], from_real[:, cells:] + from_imag[:, :cells]],
        axis=1,
    )


def half_columns(rows_own, half):
    return pl.ds(pl.multiple_of(half * rows_own, rows_own), rows_own)


def list_tiles(ids, group, starts_ref, number_ref, first_ref):
    bank, bins = starts_ref.shape[0] - 2, ids.shape[1] // lax.axis_size("rg")
    base = lax.axis_index("rg") * bins
    for number in range(bank + 1):
        before = jnp.sum((ids < number).astype(F32)).astype(jnp.int32)
        starts_ref[number] = jnp.clip(before - base, 0, bins)

    def per_filter(number, count):
        low, high = starts_ref[number], starts_ref[number + 1]
        aligned = lax.div(low, ALIGN) * ALIGN

        def per_tile(at, count):
            number_ref[count] = number
            first_ref[count] = jnp.minimum(aligned + at * group, bins - group)
            return count + 1

        tiles = jnp.where(high > low, lax.div(high - aligned + (group - 1), group), 0)
        return lax.fori_loop(0, tiles, per_tile, count)

    count = lax.fori_loop(0, bank, per_filter, 0)
    starts_ref[bank + 1] = count
    for extra in range(UNROLL - 1):
        number_ref[count + extra] = number_ref[count - 1]
        first_ref[count + extra] = first_ref[count - 1]


def prep_body(parts, group, index_any, image_any, matrix_any, *rest):
    tiles, (perm_ref, matrix_ref, begun_ref, index_ref, image_ref, tmp_ref, sems) = rest[:3], rest[3:]
    bins, rows_own = perm_ref.shape[1:]
    half = lax.axis_index("cplx")
    loads = [
        pltpu.make_async_copy(*pair, sems.at[number])
        for number, pair in enumerate(
            ((index_any, index_ref), (image_any, image_ref), (matrix_any, matrix_ref))
        )
    ]
    for load in loads:
        load.start()
    loads[0].wait()
    ids = index_ref[:, half_columns(rows_own, half)]
    rank = rank_of(ids)
    for step in range(parts):
        slot = (iota((bins, 1), 0) + part_of(parts, step) * bins).astype(F32)
        perm_ref[step] = (slot == rank).astype(BF16)
    list_tiles(ids, group, *tiles)
    loads[1].wait()
    image = split_complex(tmp_ref, image_ref[...].astype(F32))
    loads[2].wait()
    begun_ref[...] = times_image(matrix_ref, slice(None), half_columns(rows_own, half), image)


def make_bands(seg, starts_ref, table_ref, bands_ref):
    count = table_ref.shape[1] // seg
    later = iota((seg, seg), 1) >= iota((seg, seg), 0)

    def one(number):
        for part in range(2):
            row = table_ref[pl.ds(2 * number + part, 1), :]
            before = jnp.zeros((seg, seg), F32)
            columns = slice(part * seg, (part + 1) * seg)
            for block in range(count):
                same = jnp.broadcast_to(row[:, block * seg : (block + 1) * seg], (seg, seg))
                turned = pltpu.roll(same, 0, 1, stride=1, stride_axis=0)
                tile = jnp.where(later, turned, before).astype(BF16)
                bands_ref[number, (count - 1 - block) * seg : (count - block) * seg, columns] = tile
                before = turned

    def one_used(number, carry):
        pl.when(starts_ref[number + 1] > starts_ref[number])(lambda: one(number))
        return carry

    lax.fori_loop(0, bands_ref.shape[0], one_used, 0)


def fill_table(bank_ref, table_ref):
    bank, _, taps = bank_ref.shape
    table_ref[:, taps:] = jnp.zeros((2 * bank, table_ref.shape[1] - taps), F32)
    for number in range(bank):
        table_ref[2 * number : 2 * number + 2, :taps] = bank_ref[number].astype(F32)


def adjoint_bands_body(seg, starts_ref, bank_ref, bands_ref, table_ref):
    fill_table(bank_ref, table_ref)
    make_bands(seg, starts_ref, table_ref, bands_ref)


def forward_bands_body(seg, starts_ref, bank_ref, bands_ref, table_ref):
    fill_table(bank_ref, table_ref)
    taps, width = bank_ref.shape[2], table_ref.shape[1]
    turn = (iota((taps, width), 0) + iota((taps, width), 1) == taps).astype(BF16)
    table_ref[...] = mm(table_ref[:, :taps].astype(BF16), turn)
    make_bands(seg, starts_ref, table_ref, bands_ref)


def echo_body(parts, cell_count, time_any, echo_any, perm_ref, *rest):
    outs, (time_ref, echo_ref, tmp_ref, sems) = rest[:parts], rest[parts:]
    bins = perm_ref.shape[1]
    owner = lax.axis_index("az") * parts + lax.axis_index("rg")
    loads = [
        pltpu.make_async_copy(time_any, time_ref, sems.at[0]),
        pltpu.make_async_copy(echo_any, echo_ref, sems.at[1]),
    ]
    for load in loads:
        load.start()
    loads[0].wait()
    local = (time_ref[...] - owner * cell_count).astype(F32)
    slots = local.shape[1]
    hits = column_of(local) == iota((slots, cell_count), 1).astype(F32)
    place = hits.astype(BF16)
    occupied = jnp.sum(hits.astype(F32), axis=0, keepdims=True)
    loads[1].wait()
    gridded = split_complex(tmp_ref, mm(echo_ref[...], place))
    for step in range(parts):
        moved = mm(perm_ref[step], gridded).astype(BF16)
        outs[step][0:bins, :] = moved[:, :cell_count]
        outs[step][bins : 2 * bins, :] = moved[:, cell_count:]
        outs[step][2 * bins :, :] = jnp.broadcast_to(occupied, (16, cell_count)).astype(BF16)


def compress_body(step, image_ref, matrix_ref, perm_ref, begun_ref, out_ref, made_ref, tmp_ref):
    rows_own = begun_ref.shape[0]
    image = split_complex(tmp_ref, image_ref[...].astype(F32))
    columns = half_columns(rows_own, 1 - lax.axis_index("cplx"))
    made_ref[...] = (begun_ref[...] + times_image(matrix_ref, slice(None), columns, image)).astype(BF16)
    sort_body(step, made_ref, perm_ref, out_ref)


def sort_body(step, made_ref, perm_ref, out_ref):
    bins, cells = perm_ref.shape[1], made_ref.shape[1] // 2
    sent = mm(perm_ref[step], made_ref[...]).astype(BF16)
    out_ref[:bins, :] = sent[:, :cells]
    out_ref[bins:, :] = sent[:, cells:]


def sorted_matrix(parts, matrix_ref, perm_ref, columns, store):
    bins = perm_ref.shape[1]
    for step in range(parts):
        rows = pl.ds(pl.multiple_of(part_of(parts, step) * bins, bins), bins)
        for side in range(2):
            store(side, rows, mm(perm_ref[step], matrix_ref[side, :, columns]).astype(BF16))


def sort_sent_body(parts, matrix_ref, perm_ref, out_ref):
    def store(side, rows, value):
        out_ref[side, rows, :] = value

    columns = half_columns(matrix_ref.shape[1], 1 - lax.axis_index("cplx"))
    sorted_matrix(parts, matrix_ref, perm_ref, columns, store)


def fill_blocks(blocks_ref, pieces):
    for ref, at in pieces:
        if len(ref.shape) == 2:
            blocks_ref[at] = ref[...]
        else:
            for number in range(ref.shape[0]):
                blocks_ref[at + number] = ref[number]


def side_bases(parts, halo):
    even = lax.rem(lax.axis_index("az"), 2) == 0
    right = halo + parts
    return jnp.where(even, right, 0), jnp.where(even, 0, right)


def filter_groups(starts_ref, number_ref, first_ref, group, work):
    def run(chunk, carry):
        for at in range(UNROLL):
            number = number_ref[chunk * UNROLL + at]
            first = pl.multiple_of(first_ref[chunk * UNROLL + at], ALIGN)
            slot = iota((group, 1), 0) + first
            work(number, first, (slot >= starts_ref[number]) & (slot < starts_ref[number + 1]))
        return carry

    count = starts_ref[starts_ref.shape[0] - 1]
    lax.fori_loop(0, lax.div(count + (UNROLL - 1), UNROLL), run, 0)


def filtered(blocks_ref, bands, outputs, first, group, sign):
    cells, bins = blocks_ref.shape[2], blocks_ref.shape[1] // 2
    span = bands.shape[0] // cells
    rows = [
        jnp.concatenate(
            [blocks_ref[block + at, pl.ds(side * bins + first, group), :] for at in range(span)], axis=1
        )
        for block in outputs
        for side in range(2)
    ]
    made = mm(jnp.concatenate(rows, axis=0), bands)
    results = []
    for number in range(len(outputs)):
        top = made[2 * number * group : (2 * number + 1) * group]
        low = made[(2 * number + 1) * group : (2 * number + 2) * group]
        results.append(
            (top[:, :cells] - sign * low[:, cells:], low[:, :cells] + sign * top[:, cells:])
        )
    return results


def filter_all(parts, group, tiles, blocks_ref, bands_ref, sum_ref, sign):
    bins = blocks_ref.shape[1] // 2

    def work(number, first, mask):
        made = filtered(blocks_ref, bands_ref[number], range(parts), first, group, sign)
        for block in range(parts):
            for side in range(2):
                rows = pl.ds(side * bins + first, group)
                sum_ref[block, rows, :] = jnp.where(mask, made[block][side], sum_ref[block, rows, :])

    filter_groups(*tiles, group, work)


def forward_body(parts, halo, group, names, *refs):
    tiles, rest = refs[:3], refs[3:]
    count = len(names)
    pieces, bands_ref = rest[:count], rest[count]
    echoes = rest[count + 1 : -3]
    out_ref, blocks_ref, sum_ref = rest[-3:]
    bins = blocks_ref.shape[1] // 2
    even_base, odd_base = side_bases(parts, halo)
    base = {"even": even_base, "odd": odd_base, "own": halo}
    fill_blocks(
        blocks_ref,
        [
            (ref, base[side] + (part_of(parts, step) if parts == 2 else step))
            for ref, (side, step) in zip(pieces, names)
        ],
    )
    filter_all(parts, group, tiles, blocks_ref, bands_ref, sum_ref, 1.0)
    for step in range(parts):
        part = part_of(parts, step)
        echo = echoes[step][...] if len(echoes) > 1 else echoes[0][step]
        occupied = echo[2 * bins : 2 * bins + 1].astype(F32)
        model = sum_ref[part].astype(BF16).astype(F32)
        out_ref[part] = (occupied * model - echo[: 2 * bins].astype(F32)).astype(BF16)


def adjoint_body(parts, halo, group, *refs):
    tiles, (even_ref, own_ref, odd_ref, bands_ref) = refs[:3], refs[3:7]
    outs, (blocks_ref, sum_ref) = refs[7 : 7 + parts], refs[7 + parts :]
    even_base, odd_base = side_bases(parts, halo)
    fill_blocks(blocks_ref, [(even_ref, even_base), (own_ref, halo), (odd_ref, odd_base)])
    filter_all(parts, group, tiles, blocks_ref, bands_ref, sum_ref, -1.0)
    for step in range(parts):
        outs[step][...] = sum_ref[part_of(parts, step)].astype(BF16)


def turn_body(parts, matrix_ref, perm_ref, moved_ref, out_ref, sorted_ref):
    def store(side, rows, value):
        sorted_ref[side, rows, :] = value

    columns = half_columns(matrix_ref.shape[1], lax.axis_index("cplx"))
    sorted_matrix(parts, matrix_ref, perm_ref, columns, store)
    for side in range(2):
        out_ref[0, side] = sorted_ref[side].T
        out_ref[1, side] = moved_ref[side].T


def gradient_body(parts, source, step, begun, final, piece_ref, turned_ref, *refs):
    out_ref = refs[-1]
    rows_own = turned_ref.shape[2]
    cells = piece_ref.shape[-1]
    bins = rows_own // parts
    pieces = [piece_ref[...]] if len(piece_ref.shape) == 2 else [piece_ref[n] for n in range(parts)]
    both = jnp.concatenate(
        [jnp.concatenate([x[:bins], x[bins:]], axis=1) for x in pieces], axis=0
    )
    if len(pieces) > 1:
        columns = slice(None)
    else:
        columns = pl.ds(pl.multiple_of(part_of(parts, step) * bins, bins), bins)
    real, imag = [mm(turned_ref[source, side, :, columns], both) for side in range(2)]
    total = [real[:, :cells] + imag[:, cells:], real[:, cells:] - imag[:, :cells]]
    if begun:
        total = [total[0] + refs[0][:, :cells], total[1] + refs[0][:, cells:]]
    if final:
        out_ref[pl.ds(0, rows_own, stride=2), :] = total[0]
        out_ref[pl.ds(1, rows_own, stride=2), :] = total[1]
    else:
        out_ref[:, :cells] = total[0]
        out_ref[:, cells:] = total[1]


def swap_pairs(count, first):
    pairs = []
    for low in range(first, count - 1, 2):
        pairs += [(low, low + 1), (low + 1, low)]
    return pairs


def on_device(image, echoes, slot_time, range_matrix, filter_bank, filter_index):
    rows_own, _, cells = image.shape
    parts, rows_az = lax.axis_size("rg"), lax.axis_size("az")
    bins = rows_own // parts
    bank, _, taps = filter_bank.shape
    halo = taps // 2 // cells
    span = taps // cells + 1
    flip = [(0, 1), (1, 0)]
    struct = jax.ShapeDtypeStruct
    even_pairs, odd_pairs = swap_pairs(rows_az, 0), swap_pairs(rows_az, 1)

    def halves(x):
        return lax.ppermute(x, "cplx", flip)

    def share(pieces):
        if parts == 2:
            return [pieces[0], lax.ppermute(pieces[1], "rg", flip)]
        return [lax.all_to_all(jnp.stack(pieces), "rg", split_axis=0, concat_axis=0)]

    def sides(x):
        if x.ndim == 3 and x.shape[0] > halo:
            first, last = x[:halo], x[x.shape[0] - halo :]
            is_even = lax.rem(lax.axis_index("az"), 2) == 0
            to_even, to_odd = jnp.where(is_even, last, first), jnp.where(is_even, first, last)
        else:
            to_even = to_odd = x
        even = lax.ppermute(to_even, "az", even_pairs)
        odd = lax.ppermute(to_odd, "az", odd_pairs)
        return even, odd

    image_own = image.reshape(2 * rows_own, cells)
    image_other = halves(image_own)
    piece = struct((2 * bins, cells), BF16)
    in_hbm = pl.BlockSpec(memory_space=pltpu.HBM)

    def stay(*arrays):
        return [pltpu.with_memory_space_constraint(x, pltpu.HBM) for x in arrays]

    index_row = filter_index.reshape(1, filter_index.shape[0])
    split_space = pltpu.VMEM((2 * rows_own, cells), F32)
    group = min(GROUP, bins)
    tile_list = struct((bins // group + 2 * bank + UNROLL,), jnp.int32)
    *tiles, perms, matrix, begun = call(
        functools.partial(prep_body, parts, group),
        (
            struct((bank + 2,), jnp.int32),
            tile_list,
            tile_list,
            struct((parts, bins, rows_own), BF16),
            struct(range_matrix.shape, BF16),
            struct((rows_own, 2 * cells), F32),
        ),
        [in_hbm] * 3,
        [
            pltpu.VMEM(index_row.shape, jnp.int32),
            pltpu.VMEM((2 * rows_own, cells), BF16),
            split_space,
            pltpu.SemaphoreType.DMA((3,)),
        ],
        flops=8 * rows_own * rows_own * cells,
        out_specs=(SMEM, SMEM, SMEM, VMEM, VMEM, VMEM),
    )(*stay(index_row, image_own, range_matrix))
    compressed = [None] * parts
    last = parts - 1
    compressed[last], made = call(
        functools.partial(compress_body, last),
        (piece, struct((rows_own, 2 * cells), BF16)),
        [VMEM] * 4,
        [split_space],
        flops=8 * rows_own * rows_own * cells,
    )(image_other, matrix, perms, begun)
    for step in range(last):
        compressed[step] = call(
            functools.partial(sort_body, step), piece, [VMEM] * 2, flops=4 * rows_own * bins * cells
        )(made, perms)
    own = share(compressed)
    echo_pieces = call(
        functools.partial(echo_body, parts, cells),
        [struct((2 * bins + 16, cells), BF16)] * parts,
        [in_hbm] * 2 + [VMEM],
        [
            pltpu.VMEM((1, slot_time.shape[0]), jnp.int32),
            pltpu.VMEM((2 * rows_own, echoes.shape[2]), BF16),
            split_space,
            pltpu.SemaphoreType.DMA((2,)),
        ],
        flops=4 * rows_own * rows_own * cells,
    )(
        *stay(
            slot_time.reshape(1, slot_time.shape[0]),
            echoes.reshape(2 * rows_own, echoes.shape[2]),
        ),
        perms,
    )
    echo_own = share(echo_pieces)
    pieces, names = [], []
    for step, x in enumerate(own):
        even, odd = sides(x)
        pieces += [x, even, odd]
        names += [("own", step), ("even", step), ("odd", step)]
    table_space = pltpu.VMEM((2 * bank, span * cells), F32)
    bands_struct = struct((bank, span * cells, 2 * cells), BF16)
    forward_bands = call(
        functools.partial(forward_bands_body, cells),
        bands_struct,
        [SMEM, VMEM],
        [table_space],
        flops=10**9,
    )(tiles[0], filter_bank)
    moved = call(
        functools.partial(sort_sent_body, parts),
        struct((2, rows_own, rows_own), BF16),
        [VMEM] * 2,
        flops=4 * rows_own**3,
    )(matrix, perms)
    moved = halves(moved)
    filter_flops = 2 * bins * parts * 2 * span * cells * 2 * cells
    spaces = [
        pltpu.VMEM((parts + 2 * halo, 2 * bins, cells), BF16),
        pltpu.VMEM((parts, 2 * bins, cells), F32),
    ]
    residual = call(
        functools.partial(forward_body, parts, halo, group, names),
        struct((parts, 2 * bins, cells), BF16),
        [SMEM] * 3 + [VMEM] * (len(pieces) + 1 + len(echo_own)),
        spaces,
        flops=filter_flops,
    )(*tiles, *pieces, forward_bands, *echo_own)
    even, odd = sides(residual)
    adjoint_bands = call(
        functools.partial(adjoint_bands_body, cells),
        bands_struct,
        [SMEM, VMEM],
        [table_space],
        flops=10**9,
    )(tiles[0], filter_bank)
    turned = call(
        functools.partial(turn_body, parts),
        struct((2, 2, rows_own, rows_own), BF16),
        [VMEM] * 3,
        [pltpu.VMEM((2, rows_own, rows_own), BF16)],
        flops=4 * rows_own**3,
    )(matrix, perms, moved)
    back = call(
        functools.partial(adjoint_body, parts, halo, group),
        [piece] * parts,
        [SMEM] * 3 + [VMEM] * 4,
        spaces,
        flops=filter_flops,
    )(*tiles, even, residual, odd, adjoint_bands)
    back_own = share(back)
    back_other = []
    for x in back_own:
        back_other.append(halves(x))
    total = None
    for number in range(len(back_own)):
        for source, x in enumerate((back_own[number], back_other[number])):
            final = source == 1 and number == len(back_own) - 1
            args = [x, turned] + ([] if total is None else [total])
            total = call(
                functools.partial(gradient_body, parts, source, number, total is not None, final),
                struct((2 * rows_own, cells) if final else (rows_own, 2 * cells), F32),
                [VMEM] * len(args),
                flops=8 * rows_own * bins * 2 * cells,
            )(*args)
    return total.reshape(rows_own, 2, cells)


def solution(mesh):
    return jax.shard_map(
        on_device,
        mesh=mesh,
        in_specs=(
            P(("frames", "cplx"), None, ("az", "rg")),
            P(("frames", "cplx"), None, ("az", "rg")),
            P(("frames", "az", "rg")),
            P(None, "cplx", None),
            P(),
            P(),
        ),
        out_specs=P(("frames", "cplx"), None, ("az", "rg")),
        check_vma=False,
    )
```

```python
import functools

import jax
import jax.numpy as jnp
from jax import lax
from jax.experimental import pallas as pl
from jax.experimental.pallas import tpu as pltpu
from jax.sharding import PartitionSpec as P

GROUP = 48
ALIGN = 16
UNROLL = 3
FINAL_CHUNKS = 4
F32 = jnp.float32
BF16 = jnp.bfloat16
VMEM = pl.BlockSpec(memory_space=pltpu.VMEM)
SMEM = pl.BlockSpec(memory_space=pltpu.SMEM)


def mm(a, b):
    return jnp.dot(a, b, preferred_element_type=F32)


def iota(shape, axis):
    return lax.broadcasted_iota(jnp.int32, shape, axis)


def column_of(row):
    size = row.shape[1]
    eye = iota((size, size), 0) == iota((size, size), 1)
    return jnp.sum(jnp.where(eye, jnp.broadcast_to(row, (size, size)), 0.0), axis=1, keepdims=True)


def part_of(count, step):
    return lax.axis_index("rg") ^ step if count == 2 else step


def call(body, out_shape, in_specs, scratch=(), flops=0, out_specs=None, limit=None):
    count = sum(x.size * x.dtype.itemsize for x in jax.tree.leaves(out_shape))
    return pl.pallas_call(
        body,
        out_shape=out_shape,
        in_specs=in_specs,
        out_specs=jax.tree.map(lambda _: VMEM, out_shape) if out_specs is None else out_specs,
        scratch_shapes=list(scratch),
        cost_estimate=pl.CostEstimate(flops=flops, bytes_accessed=count, transcendentals=0),
        compiler_params=pltpu.CompilerParams(vmem_limit_bytes=limit or 20 * 2**20),
    )


def rank_of(ids):
    bins = ids.shape[1]
    key = (ids * bins + iota((1, bins), 1)).astype(F32)
    return jnp.sum((column_of(key) < key).astype(F32), axis=0, keepdims=True)


def split_complex(tmp_ref, values):
    bins = values.shape[0] // 2
    tmp_ref[0 : 2 * bins, :] = values
    return jnp.concatenate(
        [tmp_ref[pl.ds(0, bins, stride=2), :], tmp_ref[pl.ds(1, bins, stride=2), :]], axis=1
    ).astype(BF16)


def times_image(matrix_ref, rows, columns, image):
    cells = image.shape[1] // 2
    from_real = mm(matrix_ref[0, rows, columns], image)
    from_imag = mm(matrix_ref[1, rows, columns], image)
    return jnp.concatenate(
        [from_real[:, :cells] - from_imag[:, cells:], from_real[:, cells:] + from_imag[:, :cells]],
        axis=1,
    )


def half_columns(rows_own, half):
    return pl.ds(pl.multiple_of(half * rows_own, rows_own), rows_own)


def list_tiles(ids, group, starts_ref, number_ref, first_ref):
    bank, bins = starts_ref.shape[0] - 2, ids.shape[1] // lax.axis_size("rg")
    base = lax.axis_index("rg") * bins
    for number in range(bank + 1):
        before = jnp.sum((ids < number).astype(F32)).astype(jnp.int32)
        starts_ref[number] = jnp.clip(before - base, 0, bins)

    def per_filter(number, count):
        low, high = starts_ref[number], starts_ref[number + 1]
        aligned = lax.div(low, ALIGN) * ALIGN

        def per_tile(at, count):
            number_ref[count] = number
            first_ref[count] = jnp.minimum(aligned + at * group, bins - group)
            return count + 1

        tiles = jnp.where(high > low, lax.div(high - aligned + (group - 1), group), 0)
        return lax.fori_loop(0, tiles, per_tile, count)

    count = lax.fori_loop(0, bank, per_filter, 0)
    starts_ref[bank + 1] = count
    for extra in range(UNROLL - 1):
        number_ref[count + extra] = number_ref[count - 1]
        first_ref[count + extra] = first_ref[count - 1]


def prep_body(parts, group, index_any, image_any, matrix_any, *rest):
    tiles, (perm_ref, matrix_ref, begun_ref, index_ref, image_ref, tmp_ref, sems) = rest[:3], rest[3:]
    bins, rows_own = perm_ref.shape[1:]
    half = lax.axis_index("cplx")
    loads = [
        pltpu.make_async_copy(*pair, sems.at[number])
        for number, pair in enumerate(
            ((index_any, index_ref), (image_any, image_ref), (matrix_any, matrix_ref))
        )
    ]
    for load in loads:
        load.start()
    loads[0].wait()
    ids = index_ref[:, half_columns(rows_own, half)]
    rank = rank_of(ids)
    for step in range(parts):
        slot = (iota((bins, 1), 0) + part_of(parts, step) * bins).astype(F32)
        perm_ref[step] = (slot == rank).astype(BF16)
    list_tiles(ids, group, *tiles)
    loads[1].wait()
    image = split_complex(tmp_ref, image_ref[...].astype(F32))
    loads[2].wait()
    begun_ref[...] = times_image(matrix_ref, slice(None), half_columns(rows_own, half), image)


def make_bands(seg, starts_ref, table_ref, bands_ref):
    count = table_ref.shape[1] // seg
    later = iota((seg, seg), 1) >= iota((seg, seg), 0)

    def one(number):
        for part in range(2):
            row = table_ref[pl.ds(2 * number + part, 1), :]
            before = jnp.zeros((seg, seg), F32)
            columns = slice(part * seg, (part + 1) * seg)
            for block in range(count):
                same = jnp.broadcast_to(row[:, block * seg : (block + 1) * seg], (seg, seg))
                turned = pltpu.roll(same, 0, 1, stride=1, stride_axis=0)
                tile = jnp.where(later, turned, before).astype(BF16)
                bands_ref[number, (count - 1 - block) * seg : (count - block) * seg, columns] = tile
                before = turned

    def one_used(number, carry):
        pl.when(starts_ref[number + 1] > starts_ref[number])(lambda: one(number))
        return carry

    lax.fori_loop(0, bands_ref.shape[0], one_used, 0)


def fill_table(bank_ref, table_ref):
    bank, _, taps = bank_ref.shape
    table_ref[:, taps:] = jnp.zeros((2 * bank, table_ref.shape[1] - taps), F32)
    for number in range(bank):
        table_ref[2 * number : 2 * number + 2, :taps] = bank_ref[number].astype(F32)


def adjoint_bands_body(seg, starts_ref, bank_ref, bands_ref, table_ref):
    fill_table(bank_ref, table_ref)
    make_bands(seg, starts_ref, table_ref, bands_ref)


def forward_bands_body(seg, starts_ref, bank_ref, bands_ref, table_ref):
    fill_table(bank_ref, table_ref)
    taps, width = bank_ref.shape[2], table_ref.shape[1]
    turn = (iota((taps, width), 0) + iota((taps, width), 1) == taps).astype(BF16)
    table_ref[...] = mm(table_ref[:, :taps].astype(BF16), turn)
    make_bands(seg, starts_ref, table_ref, bands_ref)


def echo_body(parts, cell_count, time_ref, echo_ref, perm_ref, *rest):
    outs, tmp_ref = rest[:parts], rest[parts]
    bins = perm_ref.shape[1]
    owner = lax.axis_index("az") * parts + lax.axis_index("rg")
    local = (time_ref[...] - owner * cell_count).astype(F32)
    slots = local.shape[1]
    hits = column_of(local) == iota((slots, cell_count), 1).astype(F32)
    place = hits.astype(BF16)
    occupied = jnp.sum(hits.astype(F32), axis=0, keepdims=True)
    gridded = split_complex(tmp_ref, mm(echo_ref[...], place))
    for step in range(parts):
        moved = mm(perm_ref[step], gridded).astype(BF16)
        outs[step][0:bins, :] = moved[:, :cell_count]
        outs[step][bins : 2 * bins, :] = moved[:, cell_count:]
        outs[step][2 * bins :, :] = jnp.broadcast_to(occupied, (16, cell_count)).astype(BF16)


def compress_body(step, image_ref, matrix_ref, perm_ref, begun_ref, out_ref, made_ref, tmp_ref):
    rows_own = begun_ref.shape[0]
    image = split_complex(tmp_ref, image_ref[...].astype(F32))
    columns = half_columns(rows_own, 1 - lax.axis_index("cplx"))
    made_ref[...] = (begun_ref[...] + times_image(matrix_ref, slice(None), columns, image)).astype(BF16)
    sort_body(step, made_ref, perm_ref, out_ref)


def sort_body(step, made_ref, perm_ref, out_ref):
    bins, cells = perm_ref.shape[1], made_ref.shape[1] // 2
    sent = mm(perm_ref[step], made_ref[...]).astype(BF16)
    out_ref[:bins, :] = sent[:, :cells]
    out_ref[bins:, :] = sent[:, cells:]


def sorted_matrix(parts, matrix_ref, perm_ref, columns, store):
    bins = perm_ref.shape[1]
    for step in range(parts):
        rows = pl.ds(pl.multiple_of(part_of(parts, step) * bins, bins), bins)
        for side in range(2):
            store(side, rows, mm(perm_ref[step], matrix_ref[side, :, columns]).astype(BF16))


def sort_sent_body(parts, matrix_ref, perm_ref, out_ref):
    def store(side, rows, value):
        out_ref[side, rows, :] = value

    columns = half_columns(matrix_ref.shape[1], 1 - lax.axis_index("cplx"))
    sorted_matrix(parts, matrix_ref, perm_ref, columns, store)


def fill_blocks(blocks_ref, pieces):
    for ref, at in pieces:
        if len(ref.shape) == 2:
            blocks_ref[at] = ref[...]
        else:
            for number in range(ref.shape[0]):
                blocks_ref[at + number] = ref[number]


def side_bases(parts, halo):
    even = lax.rem(lax.axis_index("az"), 2) == 0
    right = halo + parts
    return jnp.where(even, right, 0), jnp.where(even, 0, right)


def filter_groups(starts_ref, number_ref, first_ref, group, work):
    def run(chunk, carry):
        for at in range(UNROLL):
            number = number_ref[chunk * UNROLL + at]
            first = pl.multiple_of(first_ref[chunk * UNROLL + at], ALIGN)
            slot = iota((group, 1), 0) + first
            work(number, first, (slot >= starts_ref[number]) & (slot < starts_ref[number + 1]))
        return carry

    count = starts_ref[starts_ref.shape[0] - 1]
    lax.fori_loop(0, lax.div(count + (UNROLL - 1), UNROLL), run, 0)


def filtered(blocks_ref, bands, outputs, first, group, sign):
    cells, bins = blocks_ref.shape[2], blocks_ref.shape[1] // 2
    span = bands.shape[0] // cells
    rows = [
        jnp.concatenate(
            [blocks_ref[block + at, pl.ds(side * bins + first, group), :] for at in range(span)], axis=1
        )
        for block in outputs
        for side in range(2)
    ]
    made = mm(jnp.concatenate(rows, axis=0), bands)
    results = []
    for number in range(len(outputs)):
        top = made[2 * number * group : (2 * number + 1) * group]
        low = made[(2 * number + 1) * group : (2 * number + 2) * group]
        results.append(
            (top[:, :cells] - sign * low[:, cells:], low[:, :cells] + sign * top[:, cells:])
        )
    return results


def filter_all(parts, group, tiles, blocks_ref, bands_ref, sum_ref, sign):
    bins = blocks_ref.shape[1] // 2

    def work(number, first, mask):
        made = filtered(blocks_ref, bands_ref[number], range(parts), first, group, sign)
        for block in range(parts):
            for side in range(2):
                rows = pl.ds(side * bins + first, group)
                sum_ref[block, rows, :] = jnp.where(mask, made[block][side], sum_ref[block, rows, :])

    filter_groups(*tiles, group, work)


def forward_body(parts, halo, group, names, *refs):
    tiles, rest = refs[:3], refs[3:]
    count = len(names)
    pieces, bands_ref = rest[:count], rest[count]
    echoes = rest[count + 1 : -3]
    out_ref, blocks_ref, sum_ref = rest[-3:]
    bins = blocks_ref.shape[1] // 2
    even_base, odd_base = side_bases(parts, halo)
    base = {"even": even_base, "odd": odd_base, "own": halo}
    fill_blocks(
        blocks_ref,
        [
            (ref, base[side] + (part_of(parts, step) if parts == 2 else step))
            for ref, (side, step) in zip(pieces, names)
        ],
    )
    filter_all(parts, group, tiles, blocks_ref, bands_ref, sum_ref, 1.0)
    for step in range(parts):
        part = part_of(parts, step)
        echo = echoes[step][...] if len(echoes) > 1 else echoes[0][step]
        occupied = echo[2 * bins : 2 * bins + 1].astype(F32)
        model = sum_ref[part].astype(BF16).astype(F32)
        out_ref[part] = (occupied * model - echo[: 2 * bins].astype(F32)).astype(BF16)


def adjoint_body(parts, halo, group, *refs):
    tiles, (even_ref, own_ref, odd_ref, bands_ref) = refs[:3], refs[3:7]
    outs, (blocks_ref, sum_ref) = refs[7 : 7 + parts], refs[7 + parts :]
    even_base, odd_base = side_bases(parts, halo)
    fill_blocks(blocks_ref, [(even_ref, even_base), (own_ref, halo), (odd_ref, odd_base)])
    filter_all(parts, group, tiles, blocks_ref, bands_ref, sum_ref, -1.0)
    for step in range(parts):
        outs[step][...] = sum_ref[part_of(parts, step)].astype(BF16)


def turn_own_body(parts, matrix_ref, perm_ref, out_ref, sorted_ref):
    def store(side, rows, value):
        sorted_ref[side, rows, :] = value

    columns = half_columns(matrix_ref.shape[1], lax.axis_index("cplx"))
    sorted_matrix(parts, matrix_ref, perm_ref, columns, store)
    for side in range(2):
        out_ref[side] = sorted_ref[side].T


def turn_other_body(moved_ref, out_ref):
    for side in range(2):
        out_ref[side] = moved_ref[side].T


def gradient_body(parts, step, begun, final, piece_ref, turned_ref, *refs):
    refs = list(refs)
    begun_ref = refs.pop(0) if begun else None
    out_ref = refs[0]
    rows_own = turned_ref.shape[1]
    cells = piece_ref.shape[-1]
    bins = rows_own // parts
    pieces = [piece_ref[...]] if len(piece_ref.shape) == 2 else [piece_ref[n] for n in range(parts)]
    both = jnp.concatenate(
        [jnp.concatenate([x[:bins], x[bins:]], axis=1) for x in pieces], axis=0
    )
    if len(pieces) > 1:
        columns = slice(None)
    else:
        columns = pl.ds(pl.multiple_of(part_of(parts, step) * bins, bins), bins)
    chunks = FINAL_CHUNKS if final else 1
    size = rows_own // chunks
    stores = []
    for chunk in range(chunks):
        rows = slice(chunk * size, (chunk + 1) * size)
        real, imag = [mm(turned_ref[side, rows, columns], both) for side in range(2)]
        total = [real[:, :cells] + imag[:, cells:], real[:, cells:] - imag[:, :cells]]
        if begun:
            total = [total[0] + begun_ref[rows, :cells], total[1] + begun_ref[rows, cells:]]
        if final:
            space_ref, sems = refs[1:]
            space_ref[pl.ds(2 * chunk * size, size, stride=2), :] = total[0]
            space_ref[pl.ds(2 * chunk * size + 1, size, stride=2), :] = total[1]
            where = pl.ds(2 * chunk * size, 2 * size)
            stores.append(
                pltpu.make_async_copy(space_ref.at[where, :], out_ref.at[where, :], sems.at[chunk])
            )
            stores[-1].start()
        else:
            out_ref[rows, :cells] = total[0]
            out_ref[rows, cells:] = total[1]
    for store in stores:
        store.wait()


def swap_pairs(count, first):
    pairs = []
    for low in range(first, count - 1, 2):
        pairs += [(low, low + 1), (low + 1, low)]
    return pairs


def on_device(image, echoes, slot_time, range_matrix, filter_bank, filter_index):
    rows_own, _, cells = image.shape
    parts, rows_az = lax.axis_size("rg"), lax.axis_size("az")
    bins = rows_own // parts
    bank, _, taps = filter_bank.shape
    halo = taps // 2 // cells
    span = taps // cells + 1
    flip = [(0, 1), (1, 0)]
    struct = jax.ShapeDtypeStruct
    even_pairs, odd_pairs = swap_pairs(rows_az, 0), swap_pairs(rows_az, 1)

    def halves(x):
        return lax.ppermute(x, "cplx", flip)

    def share(pieces):
        if parts == 2:
            return [pieces[0], lax.ppermute(pieces[1], "rg", flip)]
        return [lax.all_to_all(jnp.stack(pieces), "rg", split_axis=0, concat_axis=0)]

    def sides(x):
        if x.ndim == 3 and x.shape[0] > halo:
            first, last = x[:halo], x[x.shape[0] - halo :]
            is_even = lax.rem(lax.axis_index("az"), 2) == 0
            to_even, to_odd = jnp.where(is_even, last, first), jnp.where(is_even, first, last)
        else:
            to_even = to_odd = x
        even = lax.ppermute(to_even, "az", even_pairs)
        odd = lax.ppermute(to_odd, "az", odd_pairs)
        return even, odd

    image_own = image.reshape(2 * rows_own, cells)
    image_other = halves(image_own)
    piece = struct((2 * bins, cells), BF16)
    in_hbm = pl.BlockSpec(memory_space=pltpu.HBM)

    def stay(*arrays):
        return [pltpu.with_memory_space_constraint(x, pltpu.HBM) for x in arrays]

    index_row = filter_index.reshape(1, filter_index.shape[0])
    split_space = pltpu.VMEM((2 * rows_own, cells), F32)
    group = min(GROUP, bins)
    tile_list = struct((bins // group + 2 * bank + UNROLL,), jnp.int32)
    *tiles, perms, matrix, begun = call(
        functools.partial(prep_body, parts, group),
        (
            struct((bank + 2,), jnp.int32),
            tile_list,
            tile_list,
            struct((parts, bins, rows_own), BF16),
            struct(range_matrix.shape, BF16),
            struct((rows_own, 2 * cells), F32),
        ),
        [in_hbm] * 3,
        [
            pltpu.VMEM(index_row.shape, jnp.int32),
            pltpu.VMEM((2 * rows_own, cells), BF16),
            split_space,
            pltpu.SemaphoreType.DMA((3,)),
        ],
        flops=8 * rows_own * rows_own * cells,
        out_specs=(SMEM, SMEM, SMEM, VMEM, VMEM, VMEM),
    )(*stay(index_row, image_own, range_matrix))
    compressed = [None] * parts
    last = parts - 1
    compressed[last], made = call(
        functools.partial(compress_body, last),
        (piece, struct((rows_own, 2 * cells), BF16)),
        [VMEM] * 4,
        [split_space],
        flops=8 * rows_own * rows_own * cells,
    )(image_other, matrix, perms, begun)
    for step in range(last):
        compressed[step] = call(
            functools.partial(sort_body, step), piece, [VMEM] * 2, flops=4 * rows_own * bins * cells
        )(made, perms)
    own = share(compressed)
    echo_pieces = call(
        functools.partial(echo_body, parts, cells),
        [struct((2 * bins + 16, cells), BF16)] * parts,
        [VMEM] * 3,
        [split_space],
        flops=4 * rows_own * rows_own * cells,
    )(
        slot_time.reshape(1, slot_time.shape[0]),
        echoes.reshape(2 * rows_own, echoes.shape[2]),
        perms,
    )
    echo_own = share(echo_pieces)
    pieces, names = [], []
    for step, x in enumerate(own):
        even, odd = sides(x)
        pieces += [x, even, odd]
        names += [("own", step), ("even", step), ("odd", step)]
    table_space = pltpu.VMEM((2 * bank, span * cells), F32)
    bands_struct = struct((bank, span * cells, 2 * cells), BF16)
    forward_bands = call(
        functools.partial(forward_bands_body, cells),
        bands_struct,
        [SMEM, VMEM],
        [table_space],
        flops=10**9,
    )(tiles[0], filter_bank)
    moved = call(
        functools.partial(sort_sent_body, parts),
        struct((2, rows_own, rows_own), BF16),
        [VMEM] * 2,
        flops=4 * rows_own**3,
    )(matrix, perms)
    moved = halves(moved)
    filter_flops = 2 * bins * parts * 2 * span * cells * 2 * cells
    spaces = [
        pltpu.VMEM((parts + 2 * halo, 2 * bins, cells), BF16),
        pltpu.VMEM((parts, 2 * bins, cells), F32),
    ]
    residual = call(
        functools.partial(forward_body, parts, halo, group, names),
        struct((parts, 2 * bins, cells), BF16),
        [SMEM] * 3 + [VMEM] * (len(pieces) + 1 + len(echo_own)),
        spaces,
        flops=filter_flops,
    )(*tiles, *pieces, forward_bands, *echo_own)
    even, odd = sides(residual)
    adjoint_bands = call(
        functools.partial(adjoint_bands_body, cells),
        bands_struct,
        [SMEM, VMEM],
        [table_space],
        flops=10**9,
    )(tiles[0], filter_bank)
    square = struct((2, rows_own, rows_own), BF16)
    turned_own = call(
        functools.partial(turn_own_body, parts),
        square,
        [VMEM] * 2,
        [pltpu.VMEM(square.shape, BF16)],
        flops=4 * rows_own**3,
    )(matrix, perms)
    turned_other = call(turn_other_body, square, [VMEM], flops=10**8)(moved)
    back = call(
        functools.partial(adjoint_body, parts, halo, group),
        [piece] * parts,
        [SMEM] * 3 + [VMEM] * 4,
        spaces,
        flops=filter_flops,
    )(*tiles, even, residual, odd, adjoint_bands)
    back_own = share(back)
    back_other = []
    for x in back_own:
        back_other.append(halves(x))
    total = None
    for number in range(len(back_own)):
        for source, x in enumerate((back_own[number], back_other[number])):
            final = source == 1 and number == len(back_own) - 1
            begun = total is not None
            args = [x, (turned_own, turned_other)[source]] + ([total] if begun else [])
            shape = (2 * rows_own, cells) if final else (rows_own, 2 * cells)
            spaces = [pltpu.VMEM(shape, F32), pltpu.SemaphoreType.DMA((FINAL_CHUNKS,))]
            total = call(
                functools.partial(gradient_body, parts, number, begun, final),
                struct(shape, F32),
                [VMEM] * len(args),
                spaces if final else (),
                flops=8 * rows_own * bins * 2 * cells,
                out_specs=in_hbm if final else None,
            )(*args)
    return total.reshape(rows_own, 2, cells)


def solution(mesh):
    return jax.shard_map(
        on_device,
        mesh=mesh,
        in_specs=(
            P(("frames", "cplx"), None, ("az", "rg")),
            P(("frames", "cplx"), None, ("az", "rg")),
            P(("frames", "az", "rg")),
            P(None, "cplx", None),
            P(),
            P(),
        ),
        out_specs=P(("frames", "cplx"), None, ("az", "rg")),
        check_vma=False,
    )
```

```python
import functools

import jax
import jax.numpy as jnp
from jax import lax
from jax.experimental import pallas as pl
from jax.experimental.pallas import tpu as pltpu
from jax.sharding import PartitionSpec as P

GROUP = 48
ALIGN = 16
UNROLL = 3
FINAL_CHUNKS = 4
F32 = jnp.float32
BF16 = jnp.bfloat16
VMEM = pl.BlockSpec(memory_space=pltpu.VMEM)
SMEM = pl.BlockSpec(memory_space=pltpu.SMEM)


def mm(a, b):
    return jnp.dot(a, b, preferred_element_type=F32)


def iota(shape, axis):
    return lax.broadcasted_iota(jnp.int32, shape, axis)


def column_of(row):
    size = row.shape[1]
    eye = iota((size, size), 0) == iota((size, size), 1)
    return jnp.sum(jnp.where(eye, jnp.broadcast_to(row, (size, size)), 0.0), axis=1, keepdims=True)


def part_of(count, step):
    return lax.axis_index("rg") ^ step if count == 2 else step


def call(body, out_shape, in_specs, scratch=(), flops=0, out_specs=None, limit=None):
    count = sum(x.size * x.dtype.itemsize for x in jax.tree.leaves(out_shape))
    return pl.pallas_call(
        body,
        out_shape=out_shape,
        in_specs=in_specs,
        out_specs=jax.tree.map(lambda _: VMEM, out_shape) if out_specs is None else out_specs,
        scratch_shapes=list(scratch),
        cost_estimate=pl.CostEstimate(flops=flops, bytes_accessed=count, transcendentals=0),
        compiler_params=pltpu.CompilerParams(vmem_limit_bytes=limit or 20 * 2**20),
    )


def rank_of(ids):
    bins = ids.shape[1]
    key = (ids * bins + iota((1, bins), 1)).astype(F32)
    return jnp.sum((column_of(key) < key).astype(F32), axis=0, keepdims=True)


def split_complex(tmp_ref, values):
    bins = values.shape[0] // 2
    tmp_ref[0 : 2 * bins, :] = values
    return jnp.concatenate(
        [tmp_ref[pl.ds(0, bins, stride=2), :], tmp_ref[pl.ds(1, bins, stride=2), :]], axis=1
    ).astype(BF16)


def times_image(matrix_ref, rows, columns, image):
    cells = image.shape[1] // 2
    from_real = mm(matrix_ref[0, rows, columns], image)
    from_imag = mm(matrix_ref[1, rows, columns], image)
    return jnp.concatenate(
        [from_real[:, :cells] - from_imag[:, cells:], from_real[:, cells:] + from_imag[:, :cells]],
        axis=1,
    )


def half_columns(rows_own, half):
    return pl.ds(pl.multiple_of(half * rows_own, rows_own), rows_own)


def list_tiles(ids, group, starts_ref, number_ref, first_ref):
    bank, bins = starts_ref.shape[0] - 2, ids.shape[1] // lax.axis_size("rg")
    base = lax.axis_index("rg") * bins
    for number in range(bank + 1):
        before = jnp.sum((ids < number).astype(F32)).astype(jnp.int32)
        starts_ref[number] = jnp.clip(before - base, 0, bins)

    def per_filter(number, count):
        low, high = starts_ref[number], starts_ref[number + 1]
        aligned = lax.div(low, ALIGN) * ALIGN

        def per_tile(at, count):
            number_ref[count] = number
            first_ref[count] = jnp.minimum(aligned + at * group, bins - group)
            return count + 1

        tiles = jnp.where(high > low, lax.div(high - aligned + (group - 1), group), 0)
        return lax.fori_loop(0, tiles, per_tile, count)

    count = lax.fori_loop(0, bank, per_filter, 0)
    starts_ref[bank + 1] = count
    for extra in range(UNROLL - 1):
        number_ref[count + extra] = number_ref[count - 1]
        first_ref[count + extra] = first_ref[count - 1]


def prep_body(parts, group, index_any, image_any, matrix_any, *rest):
    tiles, (perm_ref, matrix_ref, begun_ref, index_ref, image_ref, tmp_ref, sems) = rest[:3], rest[3:]
    bins, rows_own = perm_ref.shape[1:]
    half = lax.axis_index("cplx")
    loads = [
        pltpu.make_async_copy(*pair, sems.at[number])
        for number, pair in enumerate(
            ((index_any, index_ref), (image_any, image_ref), (matrix_any, matrix_ref))
        )
    ]
    for load in loads:
        load.start()
    loads[0].wait()
    ids = index_ref[:, half_columns(rows_own, half)]
    rank = rank_of(ids)
    for step in range(parts):
        slot = (iota((bins, 1), 0) + part_of(parts, step) * bins).astype(F32)
        perm_ref[step] = (slot == rank).astype(BF16)
    list_tiles(ids, group, *tiles)
    loads[1].wait()
    image = split_complex(tmp_ref, image_ref[...].astype(F32))
    loads[2].wait()
    begun_ref[...] = times_image(matrix_ref, slice(None), half_columns(rows_own, half), image)


def make_bands(seg, starts_ref, table_ref, bands_ref):
    count = table_ref.shape[1] // seg
    later = iota((seg, seg), 1) >= iota((seg, seg), 0)

    def one(number):
        for part in range(2):
            row = table_ref[pl.ds(2 * number + part, 1), :]
            before = jnp.zeros((seg, seg), F32)
            columns = slice(part * seg, (part + 1) * seg)
            for block in range(count):
                same = jnp.broadcast_to(row[:, block * seg : (block + 1) * seg], (seg, seg))
                turned = pltpu.roll(same, 0, 1, stride=1, stride_axis=0)
                tile = jnp.where(later, turned, before).astype(BF16)
                bands_ref[number, (count - 1 - block) * seg : (count - block) * seg, columns] = tile
                before = turned

    def one_used(number, carry):
        pl.when(starts_ref[number + 1] > starts_ref[number])(lambda: one(number))
        return carry

    lax.fori_loop(0, bands_ref.shape[0], one_used, 0)


def fill_table(bank_ref, table_ref):
    bank, _, taps = bank_ref.shape
    table_ref[:, taps:] = jnp.zeros((2 * bank, table_ref.shape[1] - taps), F32)
    for number in range(bank):
        table_ref[2 * number : 2 * number + 2, :taps] = bank_ref[number].astype(F32)


def adjoint_bands_body(seg, starts_ref, bank_ref, bands_ref, table_ref):
    fill_table(bank_ref, table_ref)
    make_bands(seg, starts_ref, table_ref, bands_ref)


def forward_bands_body(seg, starts_ref, bank_ref, bands_ref, table_ref):
    fill_table(bank_ref, table_ref)
    taps, width = bank_ref.shape[2], table_ref.shape[1]
    turn = (iota((taps, width), 0) + iota((taps, width), 1) == taps).astype(BF16)
    table_ref[...] = mm(table_ref[:, :taps].astype(BF16), turn)
    make_bands(seg, starts_ref, table_ref, bands_ref)


def echo_body(parts, cell_count, time_ref, echo_ref, perm_ref, *rest):
    outs, tmp_ref = rest[:parts], rest[parts]
    bins = perm_ref.shape[1]
    owner = lax.axis_index("az") * parts + lax.axis_index("rg")
    local = (time_ref[...] - owner * cell_count).astype(F32)
    slots = local.shape[1]
    hits = column_of(local) == iota((slots, cell_count), 1).astype(F32)
    place = hits.astype(BF16)
    occupied = jnp.sum(hits.astype(F32), axis=0, keepdims=True)
    gridded = split_complex(tmp_ref, mm(echo_ref[...], place))
    for step in range(parts):
        moved = mm(perm_ref[step], gridded).astype(BF16)
        outs[step][0:bins, :] = moved[:, :cell_count]
        outs[step][bins : 2 * bins, :] = moved[:, cell_count:]
        outs[step][2 * bins :, :] = jnp.broadcast_to(occupied, (16, cell_count)).astype(BF16)


def compress_body(step, image_ref, matrix_ref, perm_ref, begun_ref, out_ref, made_ref, tmp_ref):
    rows_own = begun_ref.shape[0]
    image = split_complex(tmp_ref, image_ref[...].astype(F32))
    columns = half_columns(rows_own, 1 - lax.axis_index("cplx"))
    made_ref[...] = (begun_ref[...] + times_image(matrix_ref, slice(None), columns, image)).astype(BF16)
    sort_body(step, made_ref, perm_ref, out_ref)


def sort_body(step, made_ref, perm_ref, out_ref):
    bins, cells = perm_ref.shape[1], made_ref.shape[1] // 2
    sent = mm(perm_ref[step], made_ref[...]).astype(BF16)
    out_ref[:bins, :] = sent[:, :cells]
    out_ref[bins:, :] = sent[:, cells:]


def sorted_matrix(parts, matrix_ref, perm_ref, columns, store):
    bins = perm_ref.shape[1]
    for step in range(parts):
        rows = pl.ds(pl.multiple_of(part_of(parts, step) * bins, bins), bins)
        for side in range(2):
            store(side, rows, mm(perm_ref[step], matrix_ref[side, :, columns]).astype(BF16))


def sort_sent_body(parts, matrix_ref, perm_ref, out_ref):
    def store(side, rows, value):
        out_ref[side, rows, :] = value

    columns = half_columns(matrix_ref.shape[1], 1 - lax.axis_index("cplx"))
    sorted_matrix(parts, matrix_ref, perm_ref, columns, store)


def fill_blocks(blocks_ref, pieces):
    for ref, at in pieces:
        if len(ref.shape) == 2:
            blocks_ref[at] = ref[...]
        else:
            for number in range(ref.shape[0]):
                blocks_ref[at + number] = ref[number]


def side_bases(parts, halo):
    even = lax.rem(lax.axis_index("az"), 2) == 0
    right = halo + parts
    return jnp.where(even, right, 0), jnp.where(even, 0, right)


def filter_groups(starts_ref, number_ref, first_ref, group, work):
    def run(chunk, carry):
        for at in range(UNROLL):
            number = number_ref[chunk * UNROLL + at]
            first = pl.multiple_of(first_ref[chunk * UNROLL + at], ALIGN)
            slot = iota((group, 1), 0) + first
            work(number, first, (slot >= starts_ref[number]) & (slot < starts_ref[number + 1]))
        return carry

    count = starts_ref[starts_ref.shape[0] - 1]
    lax.fori_loop(0, lax.div(count + (UNROLL - 1), UNROLL), run, 0)


def filtered(read, cells, bins, bands, outputs, first, group, sign):
    span = bands.shape[0] // cells
    rows = [
        jnp.concatenate(
            [read(block + at, pl.ds(side * bins + first, group)) for at in range(span)], axis=1
        )
        for block in outputs
        for side in range(2)
    ]
    made = mm(jnp.concatenate(rows, axis=0), bands)
    results = []
    for number in range(len(outputs)):
        top = made[2 * number * group : (2 * number + 1) * group]
        low = made[(2 * number + 1) * group : (2 * number + 2) * group]
        results.append(
            (top[:, :cells] - sign * low[:, cells:], low[:, :cells] + sign * top[:, cells:])
        )
    return results


def filter_all(parts, group, tiles, read, bands_ref, sum_ref, sign):
    bins, cells = sum_ref.shape[1] // 2, sum_ref.shape[2]

    def work(number, first, mask):
        made = filtered(
            read, cells, bins, bands_ref[number], range(parts), first, group, sign
        )
        for block in range(parts):
            for side in range(2):
                rows = pl.ds(side * bins + first, group)
                sum_ref[block, rows, :] = jnp.where(mask, made[block][side], sum_ref[block, rows, :])

    filter_groups(*tiles, group, work)


def run_views(here, parts, group, tiles, views, bands_ref, sum_ref, sign):
    @pl.when(here)
    def _():
        filter_all(parts, group, tiles, lambda block, rows: views[block][rows, :], bands_ref, sum_ref, sign)


def forward_body(parts, halo, group, names, *refs):
    tiles, rest = refs[:3], refs[3:]
    count = len(names)
    pieces, bands_ref = rest[:count], rest[count]
    echoes = rest[count + 1 : -3]
    out_ref, blocks_ref, sum_ref = rest[-3:]
    bins = blocks_ref.shape[1] // 2
    even_base, odd_base = side_bases(parts, halo)
    base = {"even": even_base, "odd": odd_base, "own": halo}
    if parts == 2:
        for even in range(2):
            for rg in range(2):
                starts = {"even": (0, halo + parts)[even], "odd": (halo + parts, 0)[even], "own": halo}
                views = {starts[side] + (rg ^ step): ref for ref, (side, step) in zip(pieces, names)}
                here = (lax.rem(lax.axis_index("az"), 2) == 1 - even) & (lax.axis_index("rg") == rg)
                run_views(here, parts, group, tiles, views, bands_ref, sum_ref, 1.0)
    else:
        fill_blocks(blocks_ref, [(ref, base[side] + step) for ref, (side, step) in zip(pieces, names)])
        read = lambda block, rows: blocks_ref[block, rows, :]
        filter_all(parts, group, tiles, read, bands_ref, sum_ref, 1.0)
    for step in range(parts):
        part = part_of(parts, step)
        echo = echoes[step][...] if len(echoes) > 1 else echoes[0][step]
        occupied = echo[2 * bins : 2 * bins + 1].astype(F32)
        model = sum_ref[part].astype(BF16).astype(F32)
        out_ref[part] = (occupied * model - echo[: 2 * bins].astype(F32)).astype(BF16)


def adjoint_body(parts, halo, group, *refs):
    tiles, (even_ref, own_ref, odd_ref, bands_ref) = refs[:3], refs[3:7]
    outs, (blocks_ref, sum_ref) = refs[7 : 7 + parts], refs[7 + parts :]
    even_base, odd_base = side_bases(parts, halo)
    if parts == 2:
        for even in range(2):
            order = (even_ref, own_ref, odd_ref) if even == 0 else (odd_ref, own_ref, even_ref)
            slabs = [ref.at[number] for ref in order for number in range(ref.shape[0])]
            here = lax.rem(lax.axis_index("az"), 2) == 1 - even
            run_views(here, parts, group, tiles, dict(enumerate(slabs)), bands_ref, sum_ref, -1.0)
    else:
        fill_blocks(blocks_ref, [(even_ref, even_base), (own_ref, halo), (odd_ref, odd_base)])
        read = lambda block, rows: blocks_ref[block, rows, :]
        filter_all(parts, group, tiles, read, bands_ref, sum_ref, -1.0)
    for step in range(parts):
        outs[step][...] = sum_ref[part_of(parts, step)].astype(BF16)


def turn_own_body(parts, matrix_ref, perm_ref, out_ref, sorted_ref):
    def store(side, rows, value):
        sorted_ref[side, rows, :] = value

    columns = half_columns(matrix_ref.shape[1], lax.axis_index("cplx"))
    sorted_matrix(parts, matrix_ref, perm_ref, columns, store)
    for side in range(2):
        out_ref[side] = sorted_ref[side].T


def turn_other_body(moved_ref, out_ref):
    for side in range(2):
        out_ref[side] = moved_ref[side].T


def gradient_body(parts, step, begun, final, piece_ref, turned_ref, *refs):
    refs = list(refs)
    begun_ref = refs.pop(0) if begun else None
    out_ref = refs[0]
    rows_own = turned_ref.shape[1]
    cells = piece_ref.shape[-1]
    bins = rows_own // parts
    pieces = [piece_ref[...]] if len(piece_ref.shape) == 2 else [piece_ref[n] for n in range(parts)]
    both = jnp.concatenate(
        [jnp.concatenate([x[:bins], x[bins:]], axis=1) for x in pieces], axis=0
    )
    if len(pieces) > 1:
        columns = slice(None)
    else:
        columns = pl.ds(pl.multiple_of(part_of(parts, step) * bins, bins), bins)
    chunks = FINAL_CHUNKS if final else 1
    size = rows_own // chunks
    stores = []
    for chunk in range(chunks):
        rows = slice(chunk * size, (chunk + 1) * size)
        real, imag = [mm(turned_ref[side, rows, columns], both) for side in range(2)]
        total = [real[:, :cells] + imag[:, cells:], real[:, cells:] - imag[:, :cells]]
        if begun:
            total = [total[0] + begun_ref[rows, :cells], total[1] + begun_ref[rows, cells:]]
        if final:
            space_ref, sems = refs[1:]
            space_ref[pl.ds(2 * chunk * size, size, stride=2), :] = total[0]
            space_ref[pl.ds(2 * chunk * size + 1, size, stride=2), :] = total[1]
            where = pl.ds(2 * chunk * size, 2 * size)
            stores.append(
                pltpu.make_async_copy(space_ref.at[where, :], out_ref.at[where, :], sems.at[chunk])
            )
            stores[-1].start()
        else:
            out_ref[rows, :cells] = total[0]
            out_ref[rows, cells:] = total[1]
    for store in stores:
        store.wait()


def swap_pairs(count, first):
    pairs = []
    for low in range(first, count - 1, 2):
        pairs += [(low, low + 1), (low + 1, low)]
    return pairs


def on_device(image, echoes, slot_time, range_matrix, filter_bank, filter_index):
    rows_own, _, cells = image.shape
    parts, rows_az = lax.axis_size("rg"), lax.axis_size("az")
    bins = rows_own // parts
    bank, _, taps = filter_bank.shape
    halo = taps // 2 // cells
    span = taps // cells + 1
    flip = [(0, 1), (1, 0)]
    struct = jax.ShapeDtypeStruct
    even_pairs, odd_pairs = swap_pairs(rows_az, 0), swap_pairs(rows_az, 1)

    def halves(x):
        return lax.ppermute(x, "cplx", flip)

    def share(pieces):
        if parts == 2:
            return [pieces[0], lax.ppermute(pieces[1], "rg", flip)]
        return [lax.all_to_all(jnp.stack(pieces), "rg", split_axis=0, concat_axis=0)]

    def sides(x):
        if x.ndim == 3 and x.shape[0] > halo:
            first, last = x[:halo], x[x.shape[0] - halo :]
            is_even = lax.rem(lax.axis_index("az"), 2) == 0
            to_even, to_odd = jnp.where(is_even, last, first), jnp.where(is_even, first, last)
        else:
            to_even = to_odd = x
        even = lax.ppermute(to_even, "az", even_pairs)
        odd = lax.ppermute(to_odd, "az", odd_pairs)
        return even, odd

    image_own = image.reshape(2 * rows_own, cells)
    image_other = halves(image_own)
    piece = struct((2 * bins, cells), BF16)
    in_hbm = pl.BlockSpec(memory_space=pltpu.HBM)

    def stay(*arrays):
        return [pltpu.with_memory_space_constraint(x, pltpu.HBM) for x in arrays]

    index_row = filter_index.reshape(1, filter_index.shape[0])
    split_space = pltpu.VMEM((2 * rows_own, cells), F32)
    group = min(GROUP, bins)
    tile_list = struct((bins // group + 2 * bank + UNROLL,), jnp.int32)
    *tiles, perms, matrix, begun = call(
        functools.partial(prep_body, parts, group),
        (
            struct((bank + 2,), jnp.int32),
            tile_list,
            tile_list,
            struct((parts, bins, rows_own), BF16),
            struct(range_matrix.shape, BF16),
            struct((rows_own, 2 * cells), F32),
        ),
        [in_hbm] * 3,
        [
            pltpu.VMEM(index_row.shape, jnp.int32),
            pltpu.VMEM((2 * rows_own, cells), BF16),
            split_space,
            pltpu.SemaphoreType.DMA((3,)),
        ],
        flops=8 * rows_own * rows_own * cells,
        out_specs=(SMEM, SMEM, SMEM, VMEM, VMEM, VMEM),
    )(*stay(index_row, image_own, range_matrix))
    compressed = [None] * parts
    last = parts - 1
    compressed[last], made = call(
        functools.partial(compress_body, last),
        (piece, struct((rows_own, 2 * cells), BF16)),
        [VMEM] * 4,
        [split_space],
        flops=8 * rows_own * rows_own * cells,
    )(image_other, matrix, perms, begun)
    for step in range(last):
        compressed[step] = call(
            functools.partial(sort_body, step), piece, [VMEM] * 2, flops=4 * rows_own * bins * cells
        )(made, perms)
    own = share(compressed)
    echo_pieces = call(
        functools.partial(echo_body, parts, cells),
        [struct((2 * bins + 16, cells), BF16)] * parts,
        [VMEM] * 3,
        [split_space],
        flops=4 * rows_own * rows_own * cells,
    )(
        slot_time.reshape(1, slot_time.shape[0]),
        echoes.reshape(2 * rows_own, echoes.shape[2]),
        perms,
    )
    echo_own = share(echo_pieces)
    pieces, names = [], []
    for step, x in enumerate(own):
        even, odd = sides(x)
        pieces += [x, even, odd]
        names += [("own", step), ("even", step), ("odd", step)]
    table_space = pltpu.VMEM((2 * bank, span * cells), F32)
    bands_struct = struct((bank, span * cells, 2 * cells), BF16)
    forward_bands = call(
        functools.partial(forward_bands_body, cells),
        bands_struct,
        [SMEM, VMEM],
        [table_space],
        flops=10**9,
    )(tiles[0], filter_bank)
    moved = call(
        functools.partial(sort_sent_body, parts),
        struct((2, rows_own, rows_own), BF16),
        [VMEM] * 2,
        flops=4 * rows_own**3,
    )(matrix, perms)
    moved = halves(moved)
    filter_flops = 2 * bins * parts * 2 * span * cells * 2 * cells
    spaces = [
        pltpu.VMEM((parts + 2 * halo, 2 * bins, cells), BF16),
        pltpu.VMEM((parts, 2 * bins, cells), F32),
    ]
    residual = call(
        functools.partial(forward_body, parts, halo, group, names),
        struct((parts, 2 * bins, cells), BF16),
        [SMEM] * 3 + [VMEM] * (len(pieces) + 1 + len(echo_own)),
        spaces,
        flops=filter_flops,
    )(*tiles, *pieces, forward_bands, *echo_own)
    even, odd = sides(residual)
    adjoint_bands = call(
        functools.partial(adjoint_bands_body, cells),
        bands_struct,
        [SMEM, VMEM],
        [table_space],
        flops=10**9,
    )(tiles[0], filter_bank)
    square = struct((2, rows_own, rows_own), BF16)
    turned_own = call(
        functools.partial(turn_own_body, parts),
        square,
        [VMEM] * 2,
        [pltpu.VMEM(square.shape, BF16)],
        flops=4 * rows_own**3,
    )(matrix, perms)
    turned_other = call(turn_other_body, square, [VMEM], flops=10**8)(moved)
    back = call(
        functools.partial(adjoint_body, parts, halo, group),
        [piece] * parts,
        [SMEM] * 3 + [VMEM] * 4,
        spaces,
        flops=filter_flops,
    )(*tiles, even, residual, odd, adjoint_bands)
    back_own = share(back)
    back_other = []
    for x in back_own:
        back_other.append(halves(x))
    total = None
    for number in range(len(back_own)):
        for source, x in enumerate((back_own[number], back_other[number])):
            final = source == 1 and number == len(back_own) - 1
            begun = total is not None
            args = [x, (turned_own, turned_other)[source]] + ([total] if begun else [])
            shape = (2 * rows_own, cells) if final else (rows_own, 2 * cells)
            spaces = [pltpu.VMEM(shape, F32), pltpu.SemaphoreType.DMA((FINAL_CHUNKS,))]
            total = call(
                functools.partial(gradient_body, parts, number, begun, final),
                struct(shape, F32),
                [VMEM] * len(args),
                spaces if final else (),
                flops=8 * rows_own * bins * 2 * cells,
                out_specs=in_hbm if final else None,
            )(*args)
    return total.reshape(rows_own, 2, cells)


def solution(mesh):
    return jax.shard_map(
        on_device,
        mesh=mesh,
        in_specs=(
            P(("frames", "cplx"), None, ("az", "rg")),
            P(("frames", "cplx"), None, ("az", "rg")),
            P(("frames", "az", "rg")),
            P(None, "cplx", None),
            P(),
            P(),
        ),
        out_specs=P(("frames", "cplx"), None, ("az", "rg")),
        check_vma=False,
    )
```
